256 devices in a mesh: img: 64 (over x, z, core), tpa: 2 (over y_lo), tpb: 2 (over y_hi).
Axes of the slice: x: 4, y: 4 (y_hi: 2, y_lo: 2; y = y_hi * 2 + y_lo), z: 8, core: 2. Of those that a mesh axis runs over, the one named last changes fastest.
Arguments:
- images: bfloat16 [8192, 512], P('img'), may hold values from -80 to 80
- templates: bfloat16 [16384, 512], P(('tpa', 'tpb')), may hold values from -8 to 8
- rotation_index: int32 [16384], P(('tpa', 'tpb')), may hold values from 0 to 31
- tilt_index: int32 [16384], P(('tpa', 'tpb')), may hold values from 0 to 63
- inplane_index: int32 [16384], P(('tpa', 'tpb')), may hold values from 0 to 31
- image_group: int32 [8192], P('img'), may hold values from 0 to 15
- group_precision: float32 [16], replicated, may hold values from 0.5 to 2
- radius_bin: int32 [8], replicated, may hold values from 0 to 3
Outputs:
- shell_coeffs: float32 [32, 4, 2, 49], replicated
- image_loglik: float32 [8192], P('img')
The draws below stay inside these ranges and needn't reach their ends.
All inputs are finite; a program needn't handle non-finite values.
Results may differ from the reference program's by a relative error of at most 0.0024.
Values sent between devices are 32-bit elements; how exact they have to be, the bound alone decides.
A program may use at most 64 MiB of HBM per device.

```python
import math
import jax
import jax.numpy as jnp
from jax import lax

IMAGES = 8192
TEMPLATES = 16384
ORDERS = 32
RADII = 8
COEFS = 512
LDEG = 48
SHELLS = 4
NTILT = 64
NROT = 32
NPSI = 32
NGROUP = 16


def template_base(key):
    base_draw = jnp.clip(jax.random.normal(jax.random.fold_in(key, 11), (TEMPLATES, COEFS), jnp.float32), -6.0, 6.0)
    return base_draw


def draw_templates(key, part):
    return template_base(key).astype(jnp.bfloat16)


def draw_images(key, part):
    values = jnp.clip(jax.random.normal(jax.random.fold_in(key, 24), (IMAGES, COEFS), jnp.float32), -6.0, 6.0)
    return values.astype(jnp.bfloat16)


def place_ends(values, own_key, smallest, high):
    dims = values.shape
    index_at = [jax.random.randint(jax.random.fold_in(own_key, axis), (), 0, dims[axis]) for axis in range(len(dims))]
    values = values.at[tuple(index_at)].set(smallest)
    longest = dims.index(max(dims))
    index_at[longest] = (index_at[longest] + 1) % dims[longest]
    return values.at[tuple(index_at)].set(high)


def setup_inputs(seed: int = 0) -> dict:
    key_list = jax.random.split(jax.random.key(seed), 9)
    return {
        "images": draw_images(jax.random.fold_in(key_list[8], 71), 0),
        "templates": draw_templates(jax.random.fold_in(key_list[8], 71), 0),
        "rotation_index": place_ends(jax.random.randint(key_list[2], (TEMPLATES,), 0, NROT), jax.random.fold_in(key_list[2], 1), 0, NROT - 1).astype(jnp.int32),
        "tilt_index": place_ends(jax.random.randint(key_list[3], (TEMPLATES,), 0, NTILT), jax.random.fold_in(key_list[3], 1), 0, NTILT - 1).astype(jnp.int32),
        "inplane_index": place_ends(jax.random.randint(key_list[4], (TEMPLATES,), 0, NPSI), jax.random.fold_in(key_list[4], 1), 0, NPSI - 1).astype(jnp.int32),
        "image_group": place_ends(jax.random.randint(key_list[5], (IMAGES,), 0, NGROUP), jax.random.fold_in(key_list[5], 1), 0, NGROUP - 1).astype(jnp.int32),
        "group_precision": jnp.clip(jnp.exp(jax.random.uniform(key_list[6], (NGROUP,), jnp.float32, math.log(0.5), math.log(2.0))), 0.5, 2.0),
        "radius_bin": place_ends(jax.random.randint(key_list[7], (RADII,), 0, SHELLS), jax.random.fold_in(key_list[7], 1), 0, SHELLS - 1).astype(jnp.int32),
    }


RIDGE = 0.05

def legendre_table():
    angles = jnp.pi * (jnp.arange(NTILT, dtype=jnp.float32) + 0.5) / NTILT
    cosine = jnp.cos(angles)[:, None]
    sine_vals = jnp.sin(angles)
    orders_f = jnp.arange(ORDERS, dtype=jnp.float32)[None, :]
    diagonal = [jnp.full((NTILT,), (4.0 * math.pi) ** (-0.5), jnp.float32)]
    for step_m in range(1, ORDERS):
        diagonal.append(-math.sqrt((2 * step_m + 1) / (2.0 * step_m)) * sine_vals * diagonal[-1])
    corner = jnp.stack(diagonal, axis=1)
    before = jnp.zeros((NTILT, ORDERS), jnp.float32)
    latest = jnp.zeros((NTILT, ORDERS), jnp.float32)
    columns = []
    for degree in range(LDEG + 1):
        degree_f = float(degree)
        lower_f = float(degree - 1)
        factor = jnp.sqrt(max(4.0 * degree_f * degree_f - 1.0, 1.0) / jnp.maximum(degree_f * degree_f - orders_f * orders_f, 1.0))
        factor_prev = jnp.sqrt(max(4.0 * lower_f * lower_f - 1.0, 1.0) / jnp.maximum(lower_f * lower_f - orders_f * orders_f, 1.0))
        recurred = factor * (cosine * latest - before / factor_prev)
        current = jnp.where(orders_f == degree_f, corner, jnp.where(orders_f < degree_f, recurred, 0.0))
        columns.append(current)
        before, latest = (latest, current)
    return jnp.stack(columns, axis=2)

def back_project(columns, col_start, angles, tilt_hot, radius_bin, shell_table):
    pair_count = columns.shape[0] // 2
    paired = columns.reshape(pair_count, 2, columns.shape[1])
    pair_ids = col_start // 2 + jnp.arange(pair_count, dtype=jnp.int32)
    order_ids = pair_ids // RADII
    radial = pair_ids % RADII
    phases = order_ids.astype(jnp.float32)[:, None] * angles[None, :]
    cosine = jnp.cos(phases)
    sine_vals = jnp.sin(phases)
    real_y = paired[:, 0] * cosine + paired[:, 1] * sine_vals
    imag_y = paired[:, 1] * cosine - paired[:, 0] * sine_vals
    binned = jnp.dot(jnp.concatenate([real_y, imag_y], axis=0), tilt_hot, precision=lax.Precision.HIGHEST)
    order_hot = (order_ids[:, None] == jnp.arange(ORDERS, dtype=jnp.int32)[None, :]).astype(jnp.float32)
    picked = jnp.einsum('po,kol->pkl', order_hot, shell_table, precision=lax.Precision.HIGHEST)
    real_q = jnp.einsum('pk,pkl->pl', binned[:pair_count], picked, precision=lax.Precision.HIGHEST)
    imag_q = jnp.einsum('pk,pkl->pl', binned[pair_count:], picked, precision=lax.Precision.HIGHEST)
    radial_hot = radial[:, None] == jnp.arange(RADII, dtype=jnp.int32)[None, :]
    shells = lax.optimization_barrier(jnp.sum(jnp.where(radial_hot, radius_bin[None, :], 0), axis=1)).astype(jnp.int32)
    target = order_ids * SHELLS + shells
    target_hot = (target[:, None] == jnp.arange(ORDERS * SHELLS, dtype=jnp.int32)[None, :]).astype(jnp.float32)
    real_b = jnp.einsum('pg,pl->gl', target_hot, real_q, precision=lax.Precision.HIGHEST)
    imag_b = jnp.einsum('pg,pl->gl', target_hot, imag_q, precision=lax.Precision.HIGHEST)
    return jnp.stack([real_b, imag_b], axis=1).reshape(ORDERS, SHELLS, 2, LDEG + 1)

def solve_shells(right_side, bin_mass, radius_bin, shell_table):
    shell_hot = (radius_bin[:, None] == jnp.arange(SHELLS, dtype=jnp.int32)[None, :]).astype(jnp.float32)
    counts = lax.optimization_barrier(jnp.sum(shell_hot, axis=0))
    normal_m = jnp.einsum('k,kol,koj->olj', bin_mass, shell_table, shell_table, precision=lax.Precision.HIGHEST)
    ridge_term = RIDGE * jnp.mean(bin_mass)
    identity = jnp.eye(LDEG + 1, dtype=jnp.float32)
    gram = counts[None, :, None, None] * normal_m[:, None] + (ridge_term * (counts + 1.0))[None, :, None, None] * identity
    factor = jnp.linalg.cholesky(gram)
    solver = jax.vmap(jax.vmap(lambda factor_one, right_one: jax.scipy.linalg.cho_solve((factor_one, True), right_one)))
    solved = solver(factor, jnp.swapaxes(right_side, 2, 3))
    return jnp.swapaxes(solved, 2, 3) * math.sqrt(TEMPLATES)

def reference(images, templates, rotation_index, tilt_index, inplane_index, image_group, group_precision, radius_bin):
    tpl_f = templates.astype(jnp.float32)
    half_norm = 0.5 * lax.optimization_barrier(jnp.sum(tpl_f * tpl_f, axis=1))
    group_hot = image_group[:, None] == jnp.arange(NGROUP, dtype=jnp.int32)[None, :]
    weights_img = lax.optimization_barrier(jnp.sum(jnp.where(group_hot, group_precision[None, :], 0.0), axis=1)) * COEFS ** (-0.5)
    block_rows = math.gcd(IMAGES, 512)

    def step_block(carry, block_id):
        w_total, mass_total = carry
        start_row = (block_id * block_rows).astype(jnp.int32)
        img_block = lax.dynamic_slice_in_dim(images, start_row, block_rows, 0)
        weight_blk = lax.dynamic_slice_in_dim(weights_img, start_row, block_rows, 0)
        raw_dot = jnp.dot(img_block.astype(jnp.float32), templates.T.astype(jnp.float32), preferred_element_type=jnp.float32)
        scores = (raw_dot - half_norm[None, :]) * weight_blk[:, None]
        top_score = lax.optimization_barrier(jnp.max(scores, axis=1))
        log_total = top_score + jnp.log(lax.optimization_barrier(jnp.sum(jnp.exp(scores - top_score[:, None]), axis=1)))
        post_full = jnp.exp(scores - log_total[:, None])
        posterior = post_full.astype(jnp.bfloat16)
        w_total = w_total + lax.dot_general(img_block.astype(jnp.float32), posterior.astype(jnp.float32), (((0,), (0,)), ((), ())), preferred_element_type=jnp.float32)
        return ((w_total, mass_total + lax.optimization_barrier(jnp.sum(post_full, axis=0))), log_total)
    init = (jnp.zeros((COEFS, TEMPLATES), jnp.float32), jnp.zeros((TEMPLATES,), jnp.float32))
    block_ids = jnp.arange(IMAGES // block_rows, dtype=jnp.int32)
    (w_total, mass_total), log_rows = lax.scan(step_block, init, block_ids)
    image_loglik = log_rows.reshape(IMAGES)
    tilt_hot = (tilt_index[:, None] == jnp.arange(NTILT, dtype=jnp.int32)[None, :]).astype(jnp.float32)
    bin_mass = jnp.dot(mass_total, tilt_hot, precision=lax.Precision.HIGHEST)
    angles = 2.0 * jnp.pi * (rotation_index.astype(jnp.float32) / NROT + inplane_index.astype(jnp.float32) / NPSI)
    shell_table = legendre_table()
    right_side = back_project(w_total, 0, angles, tilt_hot, radius_bin, shell_table)
    return (solve_shells(right_side, bin_mass, radius_bin, shell_table), image_loglik)
```

```python
import functools
import math

import jax
import jax.numpy as jnp
import numpy as np
from jax import lax
from jax.experimental import pallas as pl
from jax.experimental.pallas import tpu as pltpu
from jax.sharding import PartitionSpec as P

TEMPLATES = 16384
ORDERS = 32
RADII = 8
COEFS = 512
LDEG = 48
SHELLS = 4
NTILT = 64
NROT = 32
NGROUP = 16
RIDGE = 0.05

NX, NZ, NCORE, NY = 4, 8, 2, 4
NYC = NY * NCORE
LANES = 128
LB = 7
LPAD = 8 * LB
LROWS = LDEG + 1
CHUNK = 256
F32, BF16, I32 = jnp.float32, jnp.bfloat16, jnp.int32
MESH = pl.DeviceIdType.MESH


def legendre_table():
    theta = np.pi * (np.arange(NTILT) + 0.5) / NTILT
    cosine, sine = np.cos(theta)[:, None], np.sin(theta)
    orders = np.arange(ORDERS, dtype=np.float64)[None, :]
    diagonal = [np.full((NTILT,), (4.0 * np.pi) ** -0.5)]
    for m in range(1, ORDERS):
        diagonal.append(-np.sqrt((2 * m + 1) / (2.0 * m)) * sine * diagonal[-1])
    corner = np.stack(diagonal, axis=1)
    before = np.zeros((NTILT, ORDERS))
    latest = np.zeros((NTILT, ORDERS))
    columns = []
    for degree in range(LDEG + 1):
        low = float(degree - 1)
        factor = np.sqrt(
            max(4.0 * degree * degree - 1.0, 1.0)
            / np.maximum(degree * degree - orders * orders, 1.0)
        )
        factor_prev = np.sqrt(
            max(4.0 * low * low - 1.0, 1.0) / np.maximum(low * low - orders * orders, 1.0)
        )
        recurred = factor * (cosine * latest - before / factor_prev)
        current = np.where(orders == degree, corner, np.where(orders < degree, recurred, 0.0))
        columns.append(current)
        before, latest = latest, current
    return np.stack(columns, axis=2)


def constant_tables():
    legendre = legendre_table().transpose(0, 2, 1)
    padded = np.zeros((NTILT, LPAD, ORDERS))
    padded[:, :LROWS] = legendre
    spread = np.tile(padded, (1, 1, SHELLS)).astype(np.float32)
    quarter = NTILT // 4
    packed = np.concatenate([padded[q * quarter : (q + 1) * quarter] for q in range(4)], axis=2)
    packed = packed.astype(np.float32)
    step = np.arange(NROT)[:, None] * np.arange(ORDERS)[None, :] % NROT
    turn = 2.0 * np.pi * step / NROT
    both = np.concatenate([np.tile(np.cos(turn), (1, 4)), np.tile(np.sin(turn), (1, 4))], axis=1)
    rest, terms = both, []
    for _ in range(3):
        term = rest.astype(np.float32).astype(jnp.bfloat16)
        terms.append(term)
        rest = rest - term.astype(np.float64)
    terms.append(np.zeros_like(terms[0]))
    phases = np.concatenate(terms, axis=0)
    return spread, packed, phases


def split2(value):
    high = value.astype(BF16)
    return high, (value - high.astype(F32)).astype(BF16)


def dot(a, b):
    return lax.dot_general(a, b, (((1,), (0,)), ((), ())), preferred_element_type=F32)


def dot_t(a, b):
    return lax.dot_general(a, b, (((1,), (1,)), ((), ())), preferred_element_type=F32)


def kernel(
    tilt_ref,
    rot_ref,
    inp_ref,
    group_ref,
    prec_ref,
    bin_ref,
    phase_ref,
    images_ref,
    lt_hbm,
    lq_hbm,
    templates_hbm,
    out_ref,
    loglik_ref,
    tpl,
    lt,
    lq,
    mlq,
    e_ref,
    ph_ref,
    emass,
    angle_t,
    cmax,
    a_ref,
    w_ref,
    pf_ref,
    dinv,
    bins_ref,
    rhs_ref,
    st_buf,
    m_yc,
    m_x,
    m_z,
    r_yc,
    r_x,
    r_z,
    r_ag,
    tpl_sem,
    tab_sem,
    st_send,
    st_recv,
    myc_send,
    myc_recv,
    mx_send,
    mx_recv,
    mz_send,
    mz_recv,
    ryc_send,
    ryc_recv,
    rx_send,
    rx_recv,
    rz_send,
    rz_recv,
    rag_send,
    rag_recv,
):
    t_count = templates_hbm.shape[0]
    chunks = t_count // CHUNK
    img = lax.axis_index("img")
    tpa = lax.axis_index("tpa")
    tpb = lax.axis_index("tpb")
    core = lax.rem(img, NCORE)
    zpos = lax.rem(lax.div(img, NCORE), NZ)
    xpos = lax.div(img, NCORE * NZ)
    ypos = tpa * 2 + tpb
    ycpos = ypos * NCORE + core

    def at_y(p):
        return {"img": img, "tpa": lax.div(p, 2), "tpb": lax.rem(p, 2)}

    def at_yc(p):
        y = lax.div(p, NCORE)
        return {
            "img": lax.div(img, NCORE) * NCORE + lax.rem(p, NCORE),
            "tpa": lax.div(y, 2),
            "tpb": lax.rem(y, 2),
        }

    def at_x(p):
        return {"img": p * (NZ * NCORE) + lax.rem(img, NZ * NCORE), "tpa": tpa, "tpb": tpb}

    def at_z(p):
        return {
            "img": lax.div(img, NZ * NCORE) * (NZ * NCORE) + p * NCORE + core,
            "tpa": tpa,
            "tpb": tpb,
        }

    def peers(n, me):
        return [lax.rem(me + d, n) for d in range(1, n)]

    def remote(src, dst, send, recv, device):
        return pltpu.make_async_remote_copy(
            src_ref=src,
            dst_ref=dst,
            send_sem=send,
            recv_sem=recv,
            device_id=device,
            device_id_type=MESH,
        )

    def share(buf, send, recv, n, me, at):
        for d, p in enumerate(peers(n, me)):
            remote(buf.at[me], buf.at[me], send.at[d], recv.at[me], at(p)).start()

    def shared(buf, send, recv, n, me, at):
        for d, p in enumerate(peers(n, me)):
            remote(buf.at[p], buf.at[p], send.at[d], recv.at[p], at(p)).wait_recv()

    def sent(buf, send, recv, n, me, at):
        for d, p in enumerate(peers(n, me)):
            remote(buf.at[me], buf.at[me], send.at[d], recv.at[me], at(p)).wait_send()

    barrier = pltpu.get_barrier_semaphore()
    for n, me, at in ((NYC, ycpos, at_yc), (NX, xpos, at_x), (NZ, zpos, at_z)):
        for p in peers(n, me):
            pl.semaphore_signal(barrier, inc=1, device_id=at(p), device_id_type=MESH)

    def tpl_copy(b):
        rows = pl.ds(pl.multiple_of(b * CHUNK, CHUNK), CHUNK)
        return pltpu.make_async_copy(templates_hbm.at[rows], tpl.at[rows], tpl_sem.at[b])

    for b in range(chunks):
        tpl_copy(b).start()
    lt_copy = pltpu.make_async_copy(lt_hbm, lt, tab_sem.at[0])
    lq_copy = pltpu.make_async_copy(lq_hbm, lq, tab_sem.at[1])
    lt_copy.start()
    lq_copy.start()

    lane = lax.broadcasted_iota(I32, (1, LANES), 1)

    group = group_ref[...]
    weight = jnp.zeros((1, LANES), F32)
    for g in range(NGROUP):
        weight = jnp.where(group == g, prec_ref[g], weight)
    weight = weight * (COEFS ** -0.5)

    c_id = lax.broadcasted_iota(I32, (COEFS, LANES), 0)
    radial = lax.rem(lax.div(c_id, 2), RADII)
    shell_of = jnp.zeros((COEFS, LANES), I32)
    for p in range(RADII):
        shell_of = jnp.where(radial == p, bin_ref[p], shell_of)
    column = shell_of * ORDERS + lax.div(c_id, 2 * RADII)
    hit = column == lax.broadcasted_iota(I32, (COEFS, LANES), 1)
    part_of = lax.rem(c_id, 2)
    select = jnp.concatenate(
        [
            jnp.where(jnp.logical_and(hit, part_of == 0), 1.0, 0.0),
            jnp.where(jnp.logical_and(hit, part_of == 1), 1.0, 0.0),
        ],
        axis=1,
    ).astype(BF16)
    images = images_ref[...]
    img_high, img_low = split2(dot(images, select))
    shelled = jnp.concatenate([img_high, img_low], axis=0)

    angle = lax.rem(rot_ref[...] + inp_ref[...], NROT).astype(F32)
    rows_t = angle.shape[0]
    angle = jnp.concatenate([angle, jnp.zeros((LANES - rows_t, LANES), F32)], axis=0)
    angle_t[...] = angle.T

    def score_chunk(b, _):
        tpl_copy(b).wait()
        rows = pl.ds(pl.multiple_of(b * CHUNK, CHUNK), CHUNK)
        block = tpl[rows, :]
        raw = dot_t(block, images)
        wide = block.astype(F32)
        half = 0.5 * jnp.sum(wide * wide, axis=1, keepdims=True)
        score = (raw - half) * weight
        top = jnp.max(score, axis=0, keepdims=True)
        e = jnp.exp(score - top)
        e_ref[rows, :] = e
        cmax[pl.ds(b, 1), :] = top
        cmax[pl.ds(chunks + b, 1), :] = jnp.sum(e, axis=0, keepdims=True)
        return 0

    lax.fori_loop(0, chunks, score_chunk, 0)

    tops = cmax[pl.ds(0, chunks), :]
    sums = cmax[pl.ds(chunks, chunks), :]
    top = jnp.max(tops, axis=0, keepdims=True)
    total = jnp.sum(sums * jnp.exp(tops - top), axis=0, keepdims=True)
    row8 = lax.broadcasted_iota(I32, (8, LANES), 0)
    st_buf[ypos] = jnp.where(row8 == 0, top, total)

    pl.semaphore_wait(barrier, (NYC - 1) + (NX - 1) + (NZ - 1))
    share(st_buf, st_send, st_recv, NY, ypos, at_y)

    def tilt_hot(b):
        tilt = jnp.concatenate(
            [tilt_ref[pl.ds(2 * b, 1), :], tilt_ref[pl.ds(2 * b + 1, 1), :]], axis=1
        )
        k_id = lax.broadcasted_iota(I32, (NTILT, CHUNK), 0)
        return jnp.where(k_id == tilt, 1.0, 0.0).astype(BF16)

    lane_sq = lax.broadcasted_iota(I32, (LANES, LANES), 1)

    def prepare_chunk(b, _):
        rows = pl.ds(pl.multiple_of(b * CHUNK, CHUNK), CHUNK)
        hots = []
        for h in range(2):
            picked = jnp.sum(
                jnp.where(lane_sq == 2 * b + h, angle_t[...], 0.0), axis=1, keepdims=True
            )
            hots.append(
                jnp.where(lax.rem(lane_sq, NROT) == picked.astype(I32), 1.0, 0.0).astype(BF16)
            )
        ph_ref[rows, :] = dot(jnp.concatenate(hots, axis=0), phase_ref[...])
        e_high, e_low = split2(e_ref[rows, :])
        both = dot(tilt_hot(b), jnp.concatenate([e_high, e_low], axis=1))
        emass[b] = both[:, :LANES] + both[:, LANES:]
        return 0

    lax.fori_loop(0, chunks, prepare_chunk, 0)

    shared(st_buf, st_send, st_recv, NY, ypos, at_y)
    stats = [st_buf[p] for p in range(NY)]
    all_top = functools.reduce(jnp.maximum, [s[0:1] for s in stats])
    all_sum = functools.reduce(
        jnp.add, [s[1:2] * jnp.exp(s[0:1] - all_top) for s in stats]
    )
    loglik = all_top + jnp.log(all_sum)
    loglik_ref[...] = loglik
    scales = jnp.exp(tops - loglik)
    cmax[pl.ds(0, chunks), :] = scales

    mass = jnp.zeros((NTILT, LANES), F32)
    for b in range(chunks):
        mass = mass + emass[b] * scales[b : b + 1]
    mass = jnp.broadcast_to(jnp.sum(mass, axis=1, keepdims=True), (NTILT, LANES))
    packed = jnp.zeros((8, LANES), F32)
    for a in range(8):
        packed = jnp.where(lax.div(lane, 16) == a, mass[8 * a : 8 * a + 8], packed)
    m_yc[ycpos] = packed
    share(m_yc, myc_send, myc_recv, NYC, ycpos, at_yc)

    bins_ref[...] = jnp.zeros_like(bins_ref)

    def post_chunk(b, _):
        rows = pl.ds(pl.multiple_of(b * CHUNK, CHUNK), CHUNK)
        posterior = (e_ref[rows, :] * cmax[pl.ds(b, 1), :]).astype(BF16)
        weighted = dot(jnp.concatenate([posterior, posterior], axis=1), shelled)
        real, imag = weighted[:, :LANES], weighted[:, LANES:]
        cosine, sine = ph_ref[rows, :LANES], ph_ref[rows, LANES:]
        rotated = jnp.concatenate(
            [real * cosine + imag * sine, imag * cosine - real * sine], axis=1
        )
        high, low = split2(rotated)
        hot = tilt_hot(b)
        both = dot(hot, high) + dot(hot, low)
        bins_ref[0] += both[:, :LANES]
        bins_ref[1] += both[:, LANES:]
        return 0

    half_way = chunks // 2
    lax.fori_loop(0, half_way, post_chunk, 0)

    shared(m_yc, myc_send, myc_recv, NYC, ycpos, at_yc)
    m_x[xpos] = functools.reduce(jnp.add, [m_yc[p] for p in range(NYC)])
    share(m_x, mx_send, mx_recv, NX, xpos, at_x)

    lax.fori_loop(half_way, chunks, post_chunk, 0)

    shared(m_x, mx_send, mx_recv, NX, xpos, at_x)
    m_z[zpos] = functools.reduce(jnp.add, [m_x[p] for p in range(NX)])
    share(m_z, mz_send, mz_recv, NZ, zpos, at_z)

    lt_copy.wait()

    def project(k8, accs):
        accs = list(accs)
        for dk in range(8):
            k = k8 * 8 + dk
            for part in range(2):
                row = bins_ref[part, pl.ds(k, 1), :]
                for jb in range(LB):
                    accs[part * LB + jb] = (
                        accs[part * LB + jb] + lt[k, 8 * jb : 8 * jb + 8, :] * row
                    )
        return tuple(accs)

    zero = jnp.zeros((8, LANES), F32)
    accs = lax.fori_loop(0, NTILT // 8, project, (zero,) * (2 * LB))
    for q in range(2 * NYC):
        rhs_ref[q // 2, (q % 2) * 8 : (q % 2) * 8 + 8, :] = accs[q] if q < 2 * LB else zero

    r_yc[ycpos] = rhs_ref[ycpos]
    for d, p in enumerate(peers(NYC, ycpos)):
        remote(
            rhs_ref.at[p], r_yc.at[ycpos], ryc_send.at[d], ryc_recv.at[ycpos], at_yc(p)
        ).start()

    lq_copy.wait()
    sub8 = lax.broadcasted_iota(I32, (8, LANES), 0)
    for jb in range(LB):
        for ib in range(LB):
            if jb <= ib:
                for r in range(8 if ib < LB - 1 else 1):
                    w_ref[ib * 8 + r, 8 * jb : 8 * jb + 8, :] = (
                        jnp.where(sub8 == r, 1.0, 0.0) if ib == jb else zero
                    )

    shared(r_yc, ryc_send, ryc_recv, NYC, ycpos, at_yc)
    r_x[xpos] = functools.reduce(jnp.add, [r_yc[p] for p in range(NYC)])
    share(r_x, rx_send, rx_recv, NX, xpos, at_x)

    shared(m_z, mz_send, mz_recv, NZ, zpos, at_z)
    pm = functools.reduce(jnp.add, [m_z[p] for p in range(NZ)])
    mean_mass = jnp.sum(jnp.sum(pm, axis=0, keepdims=True), axis=1, keepdims=True) / (
        16.0 * NTILT
    )
    first_half = lax.rem(lane, 32) < 16
    mass_h = (
        jnp.where(first_half, pm, pltpu.roll(pm, 16, 1)),
        jnp.where(first_half, pltpu.roll(pm, LANES - 16, 1), pm),
    )
    shell_lane = lax.div(lane, ORDERS)
    count = jnp.zeros((1, LANES), F32)
    for p in range(RADII):
        count = count + jnp.where(shell_lane == bin_ref[p], 1.0, 0.0)
    ridge = (RIDGE * mean_mass) * (count + 1.0)
    quarter = NTILT // 4
    for k in range(quarter):
        for jb in range(LB):
            mlq[k, 8 * jb : 8 * jb + 8, :] = (
                lq[k, 8 * jb : 8 * jb + 8, :] * mass_h[k // 8][k % 8 : k % 8 + 1]
            )
    for ib in range(LB):

        def gram_row(r, _, ib=ib):
            i = ib * 8 + r
            acc = [zero] * LB
            for k in range(quarter):
                row = mlq[k, pl.ds(i, 1), :]
                for jb in range(ib, LB):
                    acc[jb] = acc[jb] + lq[k, 8 * jb : 8 * jb + 8, :] * row
            for jb in range(ib, LB):
                v = acc[jb]
                v = v + pltpu.roll(v, 32, 1)
                v = v + pltpu.roll(v, 64, 1)
                v = v * count
                if jb == ib:
                    v = v + jnp.where(sub8 == r, ridge, 0.0)
                a_ref[i, 8 * jb : 8 * jb + 8, :] = v
            return 0

        lax.fori_loop(0, 8 if ib < LB - 1 else 1, gram_row, 0)

    shared(r_x, rx_send, rx_recv, NX, xpos, at_x)
    r_z[zpos] = functools.reduce(jnp.add, [r_x[p] for p in range(NX)])
    share(r_z, rz_send, rz_recv, NZ, zpos, at_z)

    def blk(jb):
        return slice(8 * jb, 8 * jb + 8)

    for kb in range(LB):
        rows_here = 8 if kb < LB - 1 else 1
        for kk in range(rows_here):
            k = kb * 8 + kk
            rinv = 1.0 / a_ref[k, k : k + 1, :]
            dinv[k : k + 1, :] = rinv
            if k == LDEG:
                break
            upper = {jb: a_ref[k, blk(jb), :] for jb in range(kb, LB)}
            lower = {jb: w_ref[k, blk(jb), :] for jb in range(kb + 1)}
            factor = {jb: upper[jb] * rinv for jb in range(kb, LB)}
            for jb in range(kb, LB):
                pf_ref[kk, blk(jb), :] = factor[jb]
            for ii in range(kk + 1, rows_here):
                f = factor[kb][ii : ii + 1]
                for jb in range(kb, LB):
                    a_ref[kb * 8 + ii, blk(jb), :] -= f * upper[jb]
                for jb in range(kb + 1):
                    w_ref[kb * 8 + ii, blk(jb), :] -= f * lower[jb]
        for ib in range(kb + 1, LB):

            def trail(r, _, ib=ib, kb=kb):
                i = ib * 8 + r
                f = [pf_ref[kk, pl.ds(i, 1), :] for kk in range(8)]
                for jb in range(ib, LB):
                    v = a_ref[i, blk(jb), :]
                    for kk in range(8):
                        v = v - f[kk] * a_ref[kb * 8 + kk, blk(jb), :]
                    a_ref[i, blk(jb), :] = v
                for jb in range(kb + 1):
                    v = w_ref[i, blk(jb), :]
                    for kk in range(8):
                        v = v - f[kk] * w_ref[kb * 8 + kk, blk(jb), :]
                    w_ref[i, blk(jb), :] = v
                return 0

            lax.fori_loop(0, 8 if ib < LB - 1 else 1, trail, 0)

    shared(r_z, rz_send, rz_recv, NZ, zpos, at_z)
    r_ag[ycpos] = functools.reduce(jnp.add, [r_z[p] for p in range(NZ)])
    share(r_ag, rag_send, rag_recv, NYC, ycpos, at_yc)
    shared(r_ag, rag_send, rag_recv, NYC, ycpos, at_yc)

    rhs = [r_ag[q // 2, (q % 2) * 8 : (q % 2) * 8 + 8, :] for q in range(2 * LB)]
    xs = (zero,) * (2 * LB)
    for ib in range(LB):

        def back(r, xs, ib=ib):
            i = ib * 8 + r
            xs = list(xs)
            rows = [w_ref[i, blk(jb), :] for jb in range(ib + 1)]
            d = dinv[pl.ds(i, 1), :]
            for part in range(2):
                t = rows[0] * rhs[part * LB]
                for jb in range(1, ib + 1):
                    t = t + rows[jb] * rhs[part * LB + jb]
                s = jnp.sum(t, axis=0, keepdims=True) * d
                for jb in range(ib + 1):
                    xs[part * LB + jb] = xs[part * LB + jb] + rows[jb] * s
            return tuple(xs)

        xs = lax.fori_loop(0, 8 if ib < LB - 1 else 1, back, xs)

    scale = math.sqrt(TEMPLATES)
    for part in range(2):
        full = jnp.concatenate(
            [x * scale for x in xs[part * LB : (part + 1) * LB]]
            + [jnp.zeros((LANES - LPAD, LANES), F32)],
            axis=0,
        ).T
        for s in range(SHELLS):
            out_ref[:, s, part, :] = full[s * ORDERS : (s + 1) * ORDERS, :LROWS]

    sent(st_buf, st_send, st_recv, NY, ypos, at_y)
    sent(m_yc, myc_send, myc_recv, NYC, ycpos, at_yc)
    sent(m_x, mx_send, mx_recv, NX, xpos, at_x)
    sent(m_z, mz_send, mz_recv, NZ, zpos, at_z)
    for d, p in enumerate(peers(NYC, ycpos)):
        remote(
            rhs_ref.at[p], r_yc.at[ycpos], ryc_send.at[d], ryc_recv.at[ycpos], at_yc(p)
        ).wait_send()
    sent(r_x, rx_send, rx_recv, NX, xpos, at_x)
    sent(r_z, rz_send, rz_recv, NZ, zpos, at_z)
    sent(r_ag, rag_send, rag_recv, NYC, ycpos, at_yc)


def body(images, templates, rotation, tilt, inplane, group, precision, radius_bin):
    t_count = templates.shape[0]
    rows = t_count // LANES
    chunks = t_count // CHUNK
    spread, packed, phases = constant_tables()
    vmem = pl.BlockSpec(memory_space=pltpu.VMEM)
    smem = pl.BlockSpec(memory_space=pltpu.SMEM)
    hbm = pl.BlockSpec(memory_space=pl.ANY)
    dma = pltpu.SemaphoreType.DMA
    coeffs, loglik = pl.pallas_call(
        kernel,
        out_shape=(
            jax.ShapeDtypeStruct((ORDERS, SHELLS, 2, LROWS), F32),
            jax.ShapeDtypeStruct((1, LANES), F32),
        ),
        in_specs=[vmem, vmem, vmem, vmem, smem, smem, vmem, vmem, hbm, hbm, hbm],
        out_specs=(vmem, vmem),
        scratch_shapes=[
            pltpu.VMEM((t_count, COEFS), BF16),
            pltpu.VMEM((NTILT, LPAD, LANES), F32),
            pltpu.VMEM((NTILT // 4, LPAD, LANES), F32),
            pltpu.VMEM((NTILT // 4, LPAD, LANES), F32),
            pltpu.VMEM((t_count, LANES), F32),
            pltpu.VMEM((t_count, 2 * LANES), F32),
            pltpu.VMEM((chunks, NTILT, LANES), F32),
            pltpu.VMEM((LANES, LANES), F32),
            pltpu.VMEM((2 * chunks, LANES), F32),
            pltpu.VMEM((LPAD, LPAD, LANES), F32),
            pltpu.VMEM((LPAD, LPAD, LANES), F32),
            pltpu.VMEM((8, LPAD, LANES), F32),
            pltpu.VMEM((LPAD, LANES), F32),
            pltpu.VMEM((2, NTILT, LANES), F32),
            pltpu.VMEM((NYC, 16, LANES), F32),
            pltpu.VMEM((NY, 8, LANES), F32),
            pltpu.VMEM((NYC, 8, LANES), F32),
            pltpu.VMEM((NX, 8, LANES), F32),
            pltpu.VMEM((NZ, 8, LANES), F32),
            pltpu.VMEM((NYC, 16, LANES), F32),
            pltpu.VMEM((NX, 16, LANES), F32),
            pltpu.VMEM((NZ, 16, LANES), F32),
            pltpu.VMEM((NYC, 16, LANES), F32),
            dma((chunks,)),
            dma((2,)),
            dma((NY - 1,)),
            dma((NY,)),
            dma((NYC - 1,)),
            dma((NYC,)),
            dma((NX - 1,)),
            dma((NX,)),
            dma((NZ - 1,)),
            dma((NZ,)),
            dma((NYC - 1,)),
            dma((NYC,)),
            dma((NX - 1,)),
            dma((NX,)),
            dma((NZ - 1,)),
            dma((NZ,)),
            dma((NYC - 1,)),
            dma((NYC,)),
        ],
        compiler_params=pltpu.CompilerParams(collective_id=0, has_side_effects=True),
        name="estep",
    )(
        tilt.reshape(rows, LANES),
        rotation.reshape(rows, LANES),
        inplane.reshape(rows, LANES),
        group.reshape(1, LANES),
        precision,
        radius_bin,
        jnp.asarray(phases),
        images,
        jnp.asarray(spread),
        jnp.asarray(packed),
        templates,
    )
    return coeffs, loglik.reshape(LANES)


def solution(mesh):
    in_specs = (
        P("img", None),
        P(("tpa", "tpb"), None),
        P(("tpa", "tpb")),
        P(("tpa", "tpb")),
        P(("tpa", "tpb")),
        P("img"),
        P(),
        P(),
    )
    out_specs = (P(), P("img"))
    return jax.shard_map(body, mesh=mesh, in_specs=in_specs, out_specs=out_specs, check_vma=False)
```

```python
import functools
import math

import jax
import jax.numpy as jnp
import numpy as np
from jax import lax
from jax.experimental import pallas as pl
from jax.experimental.pallas import tpu as pltpu
from jax.sharding import PartitionSpec as P

TEMPLATES = 16384
ORDERS = 32
RADII = 8
COEFS = 512
LDEG = 48
SHELLS = 4
NTILT = 64
NROT = 32
NGROUP = 16
RIDGE = 0.05
LOG2E = math.log2(math.e)

NX, NZ, NCORE, NY = 4, 8, 2, 4
NYC = NY * NCORE
HALF = NTILT // 2
LANES = 128
LB = 7
LPAD = 8 * LB
LROWS = LDEG + 1
CHUNK = 256
F32, BF16, I32 = jnp.float32, jnp.bfloat16, jnp.int32
MESH = pl.DeviceIdType.MESH


def legendre_table():
    theta = np.pi * (np.arange(NTILT) + 0.5) / NTILT
    cosine, sine = np.cos(theta)[:, None], np.sin(theta)
    orders = np.arange(ORDERS, dtype=np.float64)[None, :]
    diagonal = [np.full((NTILT,), (4.0 * np.pi) ** -0.5)]
    for m in range(1, ORDERS):
        diagonal.append(-np.sqrt((2 * m + 1) / (2.0 * m)) * sine * diagonal[-1])
    corner = np.stack(diagonal, axis=1)
    before = np.zeros((NTILT, ORDERS))
    latest = np.zeros((NTILT, ORDERS))
    columns = []
    for degree in range(LDEG + 1):
        low = float(degree - 1)
        factor = np.sqrt(
            max(4.0 * degree * degree - 1.0, 1.0)
            / np.maximum(degree * degree - orders * orders, 1.0)
        )
        factor_prev = np.sqrt(
            max(4.0 * low * low - 1.0, 1.0) / np.maximum(low * low - orders * orders, 1.0)
        )
        recurred = factor * (cosine * latest - before / factor_prev)
        current = np.where(orders == degree, corner, np.where(orders < degree, recurred, 0.0))
        columns.append(current)
        before, latest = latest, current
    return np.stack(columns, axis=2)


def constant_tables():
    legendre = legendre_table().transpose(0, 2, 1)
    padded = np.zeros((HALF, LPAD, ORDERS))
    padded[:, :LROWS] = legendre[:HALF]
    spread = np.tile(padded, (1, 1, SHELLS)).astype(np.float32)
    packed = np.concatenate([padded[q * 8 : q * 8 + 8] for q in range(4)], axis=2)
    packed = packed.astype(np.float32)
    step = np.arange(NROT)[:, None] * np.arange(ORDERS)[None, :] % NROT
    turn = 2.0 * np.pi * step / NROT
    both = np.concatenate([np.tile(np.cos(turn), (1, 4)), np.tile(np.sin(turn), (1, 4))], axis=1)
    rest, terms = both, []
    for _ in range(3):
        term = rest.astype(np.float32).astype(jnp.bfloat16)
        terms.append(term)
        rest = rest - term.astype(np.float64)
    terms.append(np.zeros_like(terms[0]))
    phases = np.concatenate(terms, axis=0)
    return spread, packed, phases


def split2(value):
    high = value.astype(BF16)
    return high, (value - high.astype(F32)).astype(BF16)


def dot(a, b):
    return lax.dot_general(a, b, (((1,), (0,)), ((), ())), preferred_element_type=F32)


def dot_t(a, b):
    return lax.dot_general(a, b, (((1,), (1,)), ((), ())), preferred_element_type=F32)


def by_two(step, count):
    def pair(i, _):
        step(2 * i)
        step(2 * i + 1)
        return 0

    lax.fori_loop(0, count // 2, pair, 0)


def kernel(
    tilt_ref,
    rot_ref,
    inp_ref,
    group_ref,
    prec_ref,
    bin_ref,
    phase_ref,
    images_ref,
    lt_hbm,
    lq_hbm,
    templates_hbm,
    out_ref,
    loglik_ref,
    tpl,
    lt,
    lq,
    mlq,
    e_ref,
    ph_ref,
    emass,
    angle_t,
    cmax,
    a_ref,
    w_ref,
    pf_ref,
    dinv,
    bins_ref,
    rhs_ref,
    st_buf,
    m_yc,
    m_x,
    m_z,
    r_yc,
    r_x,
    r_z,
    r_ag,
    tpl_sem,
    tab_sem,
    st_send,
    st_recv,
    myc_send,
    myc_recv,
    mx_send,
    mx_recv,
    mz_send,
    mz_recv,
    ryc_send,
    ryc_recv,
    rx_send,
    rx_recv,
    rz_send,
    rz_recv,
    rag_send,
    rag_recv,
):
    t_count = templates_hbm.shape[0]
    chunks = t_count // CHUNK
    img = lax.axis_index("img")
    tpa = lax.axis_index("tpa")
    tpb = lax.axis_index("tpb")
    core = lax.rem(img, NCORE)
    zpos = lax.rem(lax.div(img, NCORE), NZ)
    xpos = lax.div(img, NCORE * NZ)
    ypos = tpa * 2 + tpb
    ycpos = ypos * NCORE + core

    def at_y(p):
        return {"img": img, "tpa": lax.div(p, 2), "tpb": lax.rem(p, 2)}

    def at_yc(p):
        y = lax.div(p, NCORE)
        return {
            "img": lax.div(img, NCORE) * NCORE + lax.rem(p, NCORE),
            "tpa": lax.div(y, 2),
            "tpb": lax.rem(y, 2),
        }

    def at_x(p):
        return {"img": p * (NZ * NCORE) + lax.rem(img, NZ * NCORE), "tpa": tpa, "tpb": tpb}

    def at_z(p):
        return {
            "img": lax.div(img, NZ * NCORE) * (NZ * NCORE) + p * NCORE + core,
            "tpa": tpa,
            "tpb": tpb,
        }

    def peers(n, me):
        return [lax.rem(me + d, n) for d in range(1, n)]

    def remote(src, dst, send, recv, device):
        return pltpu.make_async_remote_copy(
            src_ref=src,
            dst_ref=dst,
            send_sem=send,
            recv_sem=recv,
            device_id=device,
            device_id_type=MESH,
        )

    def share(buf, send, recv, n, me, at):
        for d, p in enumerate(peers(n, me)):
            remote(buf.at[me], buf.at[me], send.at[d], recv.at[me], at(p)).start()

    def shared(buf, send, recv, n, me, at):
        for d, p in enumerate(peers(n, me)):
            remote(buf.at[p], buf.at[p], send.at[d], recv.at[p], at(p)).wait_recv()

    def sent(buf, send, recv, n, me, at):
        for d, p in enumerate(peers(n, me)):
            remote(buf.at[me], buf.at[me], send.at[d], recv.at[me], at(p)).wait_send()

    barrier = pltpu.get_barrier_semaphore()
    for n, me, at in ((NYC, ycpos, at_yc), (NX, xpos, at_x), (NZ, zpos, at_z)):
        for p in peers(n, me):
            pl.semaphore_signal(barrier, inc=1, device_id=at(p), device_id_type=MESH)

    def tpl_copy(b):
        rows = pl.ds(pl.multiple_of(b * 2 * CHUNK, 2 * CHUNK), 2 * CHUNK)
        return pltpu.make_async_copy(templates_hbm.at[rows], tpl.at[rows], tpl_sem.at[b])

    for b in range(chunks // 2):
        tpl_copy(b).start()
    lt_copy = pltpu.make_async_copy(lt_hbm, lt, tab_sem.at[0])
    lq_copy = pltpu.make_async_copy(lq_hbm, lq, tab_sem.at[1])
    lt_copy.start()
    lq_copy.start()

    lane = lax.broadcasted_iota(I32, (1, LANES), 1)

    group = group_ref[...]
    weight = jnp.zeros((1, LANES), F32)
    for g in range(NGROUP):
        weight = jnp.where(group == g, prec_ref[g], weight)
    weight = weight * (COEFS ** -0.5 * LOG2E)

    c_id = lax.broadcasted_iota(I32, (COEFS, LANES), 0)
    radial = lax.rem(lax.div(c_id, 2), RADII)
    shell_of = jnp.zeros((COEFS, LANES), I32)
    for p in range(RADII):
        shell_of = jnp.where(radial == p, bin_ref[p], shell_of)
    column = shell_of * ORDERS + lax.div(c_id, 2 * RADII)
    hit = column == lax.broadcasted_iota(I32, (COEFS, LANES), 1)
    part_of = lax.rem(c_id, 2)
    select = jnp.concatenate(
        [
            jnp.where(jnp.logical_and(hit, part_of == 0), 1.0, 0.0),
            jnp.where(jnp.logical_and(hit, part_of == 1), 1.0, 0.0),
        ],
        axis=1,
    ).astype(BF16)
    images = images_ref[...]
    img_high, img_low = split2(dot(images, select))
    shelled = jnp.concatenate([img_high, img_low], axis=0)

    angle = lax.rem(rot_ref[...] + inp_ref[...], NROT).astype(F32)
    rows_t = angle.shape[0]
    angle = jnp.concatenate([angle, jnp.zeros((LANES - rows_t, LANES), F32)], axis=0)
    angle_t[...] = angle.T.astype(BF16)

    def score_chunk(b):
        rows = pl.ds(pl.multiple_of(b * CHUNK, CHUNK), CHUNK)
        block = tpl[rows, :]
        raw = dot_t(block, images)
        wide = block.astype(F32)
        half = 0.5 * jnp.sum(wide * wide, axis=1, keepdims=True)
        score = (raw - half) * weight
        top = jnp.max(score, axis=0, keepdims=True)
        e = jnp.exp2(score - top)
        e_ref[rows, :] = e
        cmax[pl.ds(b, 1), :] = top
        cmax[pl.ds(chunks + b, 1), :] = jnp.sum(e, axis=0, keepdims=True)

    def score_pair(i, _):
        tpl_copy(i).wait()
        score_chunk(2 * i)
        score_chunk(2 * i + 1)
        return 0

    lax.fori_loop(0, chunks // 2, score_pair, 0)

    tops = cmax[pl.ds(0, chunks), :]
    sums = cmax[pl.ds(chunks, chunks), :]
    top = jnp.max(tops, axis=0, keepdims=True)
    total = jnp.sum(sums * jnp.exp2(tops - top), axis=0, keepdims=True)
    row8 = lax.broadcasted_iota(I32, (8, LANES), 0)
    st_buf[ypos] = jnp.where(row8 == 0, top, total)

    pl.semaphore_wait(barrier, (NYC - 1) + (NX - 1) + (NZ - 1))
    share(st_buf, st_send, st_recv, NY, ypos, at_y)

    def tilt_hot(b):
        tilt = jnp.concatenate(
            [tilt_ref[pl.ds(2 * b, 1), :], tilt_ref[pl.ds(2 * b + 1, 1), :]], axis=1
        )
        row = lax.broadcasted_iota(I32, (NTILT, CHUNK), 0)
        k_id = jnp.where(row < HALF, row, NTILT + HALF - 1 - row)
        return jnp.where(k_id == tilt, 1.0, 0.0).astype(BF16)

    row_pick = lax.broadcasted_iota(I32, (LANES, 2 * LANES), 0)
    lane_half = lax.div(lax.broadcasted_iota(I32, (LANES, 2 * LANES), 1), LANES)
    lane_turn = lax.rem(lax.broadcasted_iota(I32, (LANES, LANES), 1), NROT).astype(F32)

    def prepare_chunk(b):
        rows = pl.ds(pl.multiple_of(b * CHUNK, CHUNK), CHUNK)
        pick = jnp.where(row_pick == lane_half + 2 * b, 1.0, 0.0).astype(BF16)
        spread = dot(angle_t[...], pick)
        hots = [
            jnp.where(spread[:, h * LANES : (h + 1) * LANES] == lane_turn, 1.0, 0.0).astype(BF16)
            for h in range(2)
        ]
        ph_ref[rows, :] = dot(jnp.concatenate(hots, axis=0), phase_ref[...])
        e_high, e_low = split2(e_ref[rows, :])
        both = dot(tilt_hot(b), jnp.concatenate([e_high, e_low], axis=1))
        emass[b] = both[:, :LANES] + both[:, LANES:]

    by_two(prepare_chunk, chunks)

    shared(st_buf, st_send, st_recv, NY, ypos, at_y)
    stats = [st_buf[p] for p in range(NY)]
    all_top = functools.reduce(jnp.maximum, [s[0:1] for s in stats])
    all_sum = functools.reduce(
        jnp.add, [s[1:2] * jnp.exp2(s[0:1] - all_top) for s in stats]
    )
    log_sum = jnp.log(all_sum)
    loglik_ref[...] = all_top * math.log(2.0) + log_sum
    scales = jnp.exp2((tops - all_top) - log_sum * LOG2E)
    cmax[pl.ds(0, chunks), :] = scales

    mass = jnp.zeros((NTILT, LANES), F32)
    for b in range(chunks):
        mass = mass + emass[b] * scales[b : b + 1]
    mass = jnp.broadcast_to(jnp.sum(mass, axis=1, keepdims=True), (NTILT, LANES))
    packed = jnp.zeros((8, LANES), F32)
    for q in range(4):
        for h in range(2):
            start = h * HALF + 8 * q
            packed = jnp.where(lax.div(lane, 16) == 2 * q + h, mass[start : start + 8], packed)
    m_yc[ycpos] = packed
    share(m_yc, myc_send, myc_recv, NYC, ycpos, at_yc)

    bins_ref[...] = jnp.zeros_like(bins_ref)

    def post_chunk(i, _):
        highs, lows, hots = [], [], []
        for h in range(2):
            b = 2 * i + h
            rows = pl.ds(pl.multiple_of(b * CHUNK, CHUNK), CHUNK)
            posterior = (e_ref[rows, :] * cmax[pl.ds(b, 1), :]).astype(BF16)
            weighted = dot(jnp.concatenate([posterior, posterior], axis=1), shelled)
            real, imag = weighted[:, :LANES], weighted[:, LANES:]
            cosine, sine = ph_ref[rows, :LANES], ph_ref[rows, LANES:]
            rotated = jnp.concatenate(
                [real * cosine + imag * sine, imag * cosine - real * sine], axis=1
            )
            high, low = split2(rotated)
            highs.append(high)
            lows.append(low)
            hots.append(tilt_hot(b))
        hot = jnp.concatenate(hots, axis=1)
        both = dot(hot, jnp.concatenate(highs, axis=0)) + dot(hot, jnp.concatenate(lows, axis=0))
        bins_ref[0] += both[:, :LANES]
        bins_ref[1] += both[:, LANES:]
        return 0

    lax.fori_loop(0, chunks // 2, post_chunk, 0)

    lt_copy.wait()

    sub8 = lax.broadcasted_iota(I32, (8, LANES), 0)
    lane8 = lax.broadcasted_iota(I32, (8, LANES), 1)
    even = lax.rem(sub8 + lane8, 2) == 0

    def project(k8, accs):
        accs = list(accs)
        for dk in range(8):
            k = k8 * 8 + dk
            for part in range(2):
                row = bins_ref[part, pl.ds(k, 1), :]
                mirror = bins_ref[part, pl.ds(HALF + k, 1), :]
                folded = jnp.where(even, row + mirror, row - mirror)
                for jb in range(LB):
                    accs[part * LB + jb] = (
                        accs[part * LB + jb] + lt[k, 8 * jb : 8 * jb + 8, :] * folded
                    )
        return tuple(accs)

    zero = jnp.zeros((8, LANES), F32)
    accs = lax.fori_loop(0, HALF // 8, project, (zero,) * (2 * LB))
    for q in range(2 * NYC):
        rhs_ref[q // 2, (q % 2) * 8 : (q % 2) * 8 + 8, :] = accs[q] if q < 2 * LB else zero

    r_yc[ycpos] = rhs_ref[ycpos]
    for d, p in enumerate(peers(NYC, ycpos)):
        remote(
            rhs_ref.at[p], r_yc.at[ycpos], ryc_send.at[d], ryc_recv.at[ycpos], at_yc(p)
        ).start()

    shared(m_yc, myc_send, myc_recv, NYC, ycpos, at_yc)
    m_x[xpos] = functools.reduce(jnp.add, [m_yc[p] for p in range(NYC)])
    share(m_x, mx_send, mx_recv, NX, xpos, at_x)

    lq_copy.wait()
    for jb in range(LB):
        for ib in range(LB):
            if jb <= ib:
                for r in range(8 if ib < LB - 1 else 1):
                    w_ref[ib * 8 + r, 8 * jb : 8 * jb + 8, :] = (
                        jnp.where(sub8 == r, 1.0, 0.0) if ib == jb else zero
                    )

    shared(r_yc, ryc_send, ryc_recv, NYC, ycpos, at_yc)
    r_x[xpos] = functools.reduce(jnp.add, [r_yc[p] for p in range(NYC)])
    share(r_x, rx_send, rx_recv, NX, xpos, at_x)

    shared(m_x, mx_send, mx_recv, NX, xpos, at_x)
    m_z[zpos] = functools.reduce(jnp.add, [m_x[p] for p in range(NX)])
    share(m_z, mz_send, mz_recv, NZ, zpos, at_z)

    shared(r_x, rx_send, rx_recv, NX, xpos, at_x)
    r_z[zpos] = functools.reduce(jnp.add, [r_x[p] for p in range(NX)])
    share(r_z, rz_send, rz_recv, NZ, zpos, at_z)

    shared(m_z, mz_send, mz_recv, NZ, zpos, at_z)
    pm = functools.reduce(jnp.add, [m_z[p] for p in range(NZ)])
    mean_mass = jnp.sum(jnp.sum(pm, axis=0, keepdims=True), axis=1, keepdims=True) / (
        16.0 * NTILT
    )
    first_half = lax.rem(lane, 32) < 16
    near = jnp.where(first_half, pm, pltpu.roll(pm, 16, 1))
    far = jnp.where(first_half, pltpu.roll(pm, LANES - 16, 1), pm)
    both_mass, diff_mass = near + far, near - far
    shell_lane = lax.div(lane, ORDERS)
    count = jnp.zeros((1, LANES), F32)
    for p in range(RADII):
        count = count + jnp.where(shell_lane == bin_ref[p], 1.0, 0.0)
    ridge = (RIDGE * mean_mass) * (count + 1.0)
    sub_even = lax.rem(sub8, 2) == 0
    for k in range(8):
        plus, minus = both_mass[k : k + 1], diff_mass[k : k + 1]
        for parity in range(2):
            signed = jnp.where(sub_even, minus, plus) if parity else jnp.where(sub_even, plus, minus)
            for jb in range(LB):
                mlq[parity * 8 + k, 8 * jb : 8 * jb + 8, :] = (
                    lq[k, 8 * jb : 8 * jb + 8, :] * signed
                )
    for ib in range(LB):

        def gram_rows(h, _, ib=ib):
            group = 4 if ib < LB - 1 else 1
            first = ib * 8 + h * 4
            acc = [[zero] * LB for _ in range(group)]
            for k in range(8):
                rows = [lq[k, pl.ds(first + r, 1), :] for r in range(group)]
                for jb in range(ib, LB):
                    for parity in range(min(group, 2)):
                        term = mlq[parity * 8 + k, 8 * jb : 8 * jb + 8, :]
                        for r in range(parity, group, 2):
                            acc[r][jb] = acc[r][jb] + term * rows[r]
            for jb in range(ib, LB):
                for r in range(group):
                    v = acc[r][jb]
                    v = v + pltpu.roll(v, 32, 1)
                    v = v + pltpu.roll(v, 64, 1)
                    v = v * count
                    if jb == ib:
                        v = v + jnp.where(sub8 == h * 4 + r, ridge, 0.0)
                    a_ref[first + r, 8 * jb : 8 * jb + 8, :] = v
            return 0

        lax.fori_loop(0, 2 if ib < LB - 1 else 1, gram_rows, 0)

    def blk(jb):
        return slice(8 * jb, 8 * jb + 8)

    for kb in range(LB):
        rows_here = 8 if kb < LB - 1 else 1
        for kk in range(rows_here):
            k = kb * 8 + kk
            rinv = 1.0 / a_ref[k, k : k + 1, :]
            dinv[k : k + 1, :] = rinv
            if k == LDEG:
                break
            upper = {jb: a_ref[k, blk(jb), :] for jb in range(kb, LB)}
            lower = {jb: w_ref[k, blk(jb), :] for jb in range(kb + 1)}
            factor = {jb: upper[jb] * rinv for jb in range(kb, LB)}
            for jb in range(kb, LB):
                pf_ref[kk, blk(jb), :] = factor[jb]
            for ii in range(kk + 1, rows_here):
                f = factor[kb][ii : ii + 1]
                for jb in range(kb, LB):
                    a_ref[kb * 8 + ii, blk(jb), :] -= f * upper[jb]
                for jb in range(kb + 1):
                    w_ref[kb * 8 + ii, blk(jb), :] -= f * lower[jb]
        for ib in range(kb + 1, LB):

            def trail(h, _, ib=ib, kb=kb):
                group = 4 if ib < LB - 1 else 1
                first = ib * 8 + h * 4
                f = [
                    [pf_ref[kk, pl.ds(first + r, 1), :] for r in range(group)] for kk in range(8)
                ]
                for ref, blocks in ((a_ref, range(ib, LB)), (w_ref, range(kb + 1))):
                    for jb in blocks:
                        v = [ref[first + r, blk(jb), :] for r in range(group)]
                        for kk in range(8):
                            u = ref[kb * 8 + kk, blk(jb), :]
                            v = [v[r] - f[kk][r] * u for r in range(group)]
                        for r in range(group):
                            ref[first + r, blk(jb), :] = v[r]
                return 0

            lax.fori_loop(0, 2 if ib < LB - 1 else 1, trail, 0)
        if kb == 1:
            shared(r_z, rz_send, rz_recv, NZ, zpos, at_z)
            r_ag[ycpos] = functools.reduce(jnp.add, [r_z[p] for p in range(NZ)])
            share(r_ag, rag_send, rag_recv, NYC, ycpos, at_yc)

    sent(st_buf, st_send, st_recv, NY, ypos, at_y)
    sent(m_yc, myc_send, myc_recv, NYC, ycpos, at_yc)
    sent(m_x, mx_send, mx_recv, NX, xpos, at_x)
    sent(m_z, mz_send, mz_recv, NZ, zpos, at_z)
    for d, p in enumerate(peers(NYC, ycpos)):
        remote(
            rhs_ref.at[p], r_yc.at[ycpos], ryc_send.at[d], ryc_recv.at[ycpos], at_yc(p)
        ).wait_send()
    sent(r_x, rx_send, rx_recv, NX, xpos, at_x)
    sent(r_z, rz_send, rz_recv, NZ, zpos, at_z)
    shared(r_ag, rag_send, rag_recv, NYC, ycpos, at_yc)

    rhs = [r_ag[q // 2, (q % 2) * 8 : (q % 2) * 8 + 8, :] for q in range(2 * LB)]
    xs = (zero,) * (2 * LB)
    for ib in range(LB):

        def back(r, xs, ib=ib):
            i = ib * 8 + r
            xs = list(xs)
            rows = [w_ref[i, blk(jb), :] for jb in range(ib + 1)]
            d = dinv[pl.ds(i, 1), :]
            for part in range(2):
                t = rows[0] * rhs[part * LB]
                for jb in range(1, ib + 1):
                    t = t + rows[jb] * rhs[part * LB + jb]
                s = jnp.sum(t, axis=0, keepdims=True) * d
                for jb in range(ib + 1):
                    xs[part * LB + jb] = xs[part * LB + jb] + rows[jb] * s
            return tuple(xs)

        xs = lax.fori_loop(0, 8 if ib < LB - 1 else 1, back, xs)

    scale = math.sqrt(TEMPLATES)
    for q in range(2 * LB):
        out_ref[q // LB, blk(q % LB), :] = xs[q] * scale

    sent(r_ag, rag_send, rag_recv, NYC, ycpos, at_yc)


def arrange(x_ref, row_ref, out_ref, loglik_ref):
    loglik_ref[...] = row_ref[...]
    pad = jnp.zeros((LANES - LPAD, LANES), F32)
    for part in range(2):
        full = jnp.concatenate([x_ref[part], pad], axis=0).T
        for s in range(SHELLS):
            out_ref[:, s, part, :] = full[s * ORDERS : (s + 1) * ORDERS, :LROWS]


def body(images, templates, rotation, tilt, inplane, group, precision, radius_bin):
    t_count = templates.shape[0]
    rows = t_count // LANES
    chunks = t_count // CHUNK
    spread, packed, phases = constant_tables()
    vmem = pl.BlockSpec(memory_space=pltpu.VMEM)
    smem = pl.BlockSpec(memory_space=pltpu.SMEM)
    hbm = pl.BlockSpec(memory_space=pl.ANY)
    dma = pltpu.SemaphoreType.DMA
    solved, row = pl.pallas_call(
        kernel,
        out_shape=(
            jax.ShapeDtypeStruct((2, LPAD, LANES), F32),
            jax.ShapeDtypeStruct((1, LANES), F32),
        ),
        in_specs=[vmem, vmem, vmem, vmem, smem, smem, vmem, vmem, hbm, hbm, hbm],
        out_specs=(vmem, vmem),
        scratch_shapes=[
            pltpu.VMEM((t_count, COEFS), BF16),
            pltpu.VMEM((HALF, LPAD, LANES), F32),
            pltpu.VMEM((8, LPAD, LANES), F32),
            pltpu.VMEM((16, LPAD, LANES), F32),
            pltpu.VMEM((t_count, LANES), F32),
            pltpu.VMEM((t_count, 2 * LANES), F32),
            pltpu.VMEM((chunks, NTILT, LANES), F32),
            pltpu.VMEM((LANES, LANES), BF16),
            pltpu.VMEM((2 * chunks, LANES), F32),
            pltpu.VMEM((LPAD, LPAD, LANES), F32),
            pltpu.VMEM((LPAD, LPAD, LANES), F32),
            pltpu.VMEM((8, LPAD, LANES), F32),
            pltpu.VMEM((LPAD, LANES), F32),
            pltpu.VMEM((2, NTILT, LANES), F32),
            pltpu.VMEM((NYC, 16, LANES), F32),
            pltpu.VMEM((NY, 8, LANES), F32),
            pltpu.VMEM((NYC, 8, LANES), F32),
            pltpu.VMEM((NX, 8, LANES), F32),
            pltpu.VMEM((NZ, 8, LANES), F32),
            pltpu.VMEM((NYC, 16, LANES), F32),
            pltpu.VMEM((NX, 16, LANES), F32),
            pltpu.VMEM((NZ, 16, LANES), F32),
            pltpu.VMEM((NYC, 16, LANES), F32),
            dma((chunks // 2,)),
            dma((2,)),
            dma((NY - 1,)),
            dma((NY,)),
            dma((NYC - 1,)),
            dma((NYC,)),
            dma((NX - 1,)),
            dma((NX,)),
            dma((NZ - 1,)),
            dma((NZ,)),
            dma((NYC - 1,)),
            dma((NYC,)),
            dma((NX - 1,)),
            dma((NX,)),
            dma((NZ - 1,)),
            dma((NZ,)),
            dma((NYC - 1,)),
            dma((NYC,)),
        ],
        compiler_params=pltpu.CompilerParams(collective_id=0, has_side_effects=True),
        name="estep",
    )(
        tilt.reshape(rows, LANES),
        rotation.reshape(rows, LANES),
        inplane.reshape(rows, LANES),
        group.reshape(1, LANES),
        precision,
        radius_bin,
        jnp.asarray(phases),
        images,
        jnp.asarray(spread),
        jnp.asarray(packed),
        templates,
    )
    coeffs, loglik = pl.pallas_call(
        arrange,
        out_shape=(
            jax.ShapeDtypeStruct((ORDERS, SHELLS, 2, LROWS), F32),
            jax.ShapeDtypeStruct((1, LANES), F32),
        ),
        in_specs=[vmem, vmem],
        out_specs=(vmem, vmem),
        name="arrange",
    )(solved, row)
    return coeffs, loglik.reshape(LANES)


def solution(mesh):
    in_specs = (
        P("img", None),
        P(("tpa", "tpb"), None),
        P(("tpa", "tpb")),
        P(("tpa", "tpb")),
        P(("tpa", "tpb")),
        P("img"),
        P(),
        P(),
    )
    out_specs = (P(), P("img"))
    return jax.shard_map(body, mesh=mesh, in_specs=in_specs, out_specs=out_specs, check_vma=False)
```

```python
import functools
import math

import jax
import jax.numpy as jnp
import numpy as np
from jax import lax
from jax.experimental import pallas as pl
from jax.experimental.pallas import tpu as pltpu
from jax.sharding import PartitionSpec as P

TEMPLATES = 16384
ORDERS = 32
RADII = 8
COEFS = 512
LDEG = 48
SHELLS = 4
NTILT = 64
NROT = 32
NGROUP = 16
RIDGE = 0.05
LOG2E = math.log2(math.e)

NX, NZ, NCORE, NY = 4, 8, 2, 4
NYC = NY * NCORE
NZC = NZ * NCORE
NXY = NX * NY
HALF = NTILT // 2
LANES = 128
LB = 7
LPAD = 8 * LB
LROWS = LDEG + 1
CHUNK = 512
CUTS = CHUNK // LANES
F32, BF16, I32 = jnp.float32, jnp.bfloat16, jnp.int32
MESH = pl.DeviceIdType.MESH


def legendre_table():
    theta = np.pi * (np.arange(NTILT) + 0.5) / NTILT
    cosine, sine = np.cos(theta)[:, None], np.sin(theta)
    orders = np.arange(ORDERS, dtype=np.float64)[None, :]
    diagonal = [np.full((NTILT,), (4.0 * np.pi) ** -0.5)]
    for m in range(1, ORDERS):
        diagonal.append(-np.sqrt((2 * m + 1) / (2.0 * m)) * sine * diagonal[-1])
    corner = np.stack(diagonal, axis=1)
    before = np.zeros((NTILT, ORDERS))
    latest = np.zeros((NTILT, ORDERS))
    columns = []
    for degree in range(LDEG + 1):
        low = float(degree - 1)
        factor = np.sqrt(
            max(4.0 * degree * degree - 1.0, 1.0)
            / np.maximum(degree * degree - orders * orders, 1.0)
        )
        factor_prev = np.sqrt(
            max(4.0 * low * low - 1.0, 1.0) / np.maximum(low * low - orders * orders, 1.0)
        )
        recurred = factor * (cosine * latest - before / factor_prev)
        current = np.where(orders == degree, corner, np.where(orders < degree, recurred, 0.0))
        columns.append(current)
        before, latest = latest, current
    return np.stack(columns, axis=2)


def constant_tables():
    legendre = legendre_table().transpose(0, 2, 1)
    padded = np.zeros((HALF, LPAD, ORDERS))
    padded[:, :LROWS] = legendre[:HALF]
    spread = np.tile(padded, (1, 1, SHELLS)).astype(np.float32)
    packed = np.concatenate([padded[q * 8 : q * 8 + 8] for q in range(4)], axis=2)
    packed = packed.astype(np.float32)
    step = np.arange(NROT)[:, None] * np.arange(ORDERS)[None, :] % NROT
    turn = 2.0 * np.pi * step / NROT
    both = np.concatenate([np.tile(np.cos(turn), (1, 4)), np.tile(np.sin(turn), (1, 4))], axis=1)
    rest, terms = both, []
    for _ in range(3):
        term = rest.astype(np.float32).astype(jnp.bfloat16)
        terms.append(term)
        rest = rest - term.astype(np.float64)
    terms.append(np.zeros_like(terms[0]))
    phases = np.concatenate(terms, axis=0)
    return spread, packed, phases


def split2(value):
    high = value.astype(BF16)
    return high, (value - high.astype(F32)).astype(BF16)


def dot(a, b):
    return lax.dot_general(a, b, (((1,), (0,)), ((), ())), preferred_element_type=F32)


def dot_t(a, b):
    return lax.dot_general(a, b, (((1,), (1,)), ((), ())), preferred_element_type=F32)


def kernel(
    tilt_hbm,
    rot_hbm,
    inp_hbm,
    group_ref,
    prec_ref,
    bin_ref,
    phase_hbm,
    images_hbm,
    lt_hbm,
    lq_hbm,
    templates_hbm,
    out_ref,
    loglik_ref,
    tilt_ref,
    rot_ref,
    inp_ref,
    phase_ref,
    images_ref,
    raw_buf,
    score_buf,
    high_buf,
    low_buf,
    tpl,
    lt,
    lq,
    mlq,
    e_ref,
    ph_ref,
    emass,
    angle_t,
    cmax,
    a_ref,
    w_ref,
    pf_ref,
    dinv,
    bins_ref,
    rhs_ref,
    st_buf,
    m_zc,
    m_xy,
    r_yc,
    r_x,
    r_z,
    r_ag,
    tpl_sem,
    tab_sem,
    st_send,
    st_recv,
    mzc_send,
    mzc_recv,
    mxy_send,
    mxy_recv,
    ryc_send,
    ryc_recv,
    rx_send,
    rx_recv,
    rz_send,
    rz_recv,
    rag_send,
    rag_recv,
):
    t_count = templates_hbm.shape[0]
    chunks = t_count // CHUNK
    img = lax.axis_index("img")
    tpa = lax.axis_index("tpa")
    tpb = lax.axis_index("tpb")
    core = lax.rem(img, NCORE)
    zpos = lax.rem(lax.div(img, NCORE), NZ)
    xpos = lax.div(img, NCORE * NZ)
    ypos = tpa * 2 + tpb
    ycpos = core * NY + ypos

    zcpos = zpos * NCORE + core
    xypos = xpos * NY + ypos
    chip = img - core
    column = img - zcpos

    def device(at_img, y):
        return {"img": at_img, "tpa": lax.div(y, 2), "tpb": lax.rem(y, 2)}

    def at_y(p):
        return device(img, p)

    def at_yc(p):
        return device(chip + lax.div(p, NY), lax.rem(p, NY))

    def at_x(p):
        return {"img": p * NZC + zcpos, "tpa": tpa, "tpb": tpb}

    def at_z(p):
        return {"img": column + p * NCORE + core, "tpa": tpa, "tpb": tpb}

    def at_zc(p):
        return {"img": column + p, "tpa": tpa, "tpb": tpb}

    def at_xy(p):
        return device(lax.div(p, NY) * NZC + zcpos, lax.rem(p, NY))

    def peers(n, me):
        return [lax.rem(me + d, n) for d in range(1, n)]

    def remote(src, dst, send, recv, device):
        return pltpu.make_async_remote_copy(
            src_ref=src,
            dst_ref=dst,
            send_sem=send,
            recv_sem=recv,
            device_id=device,
            device_id_type=MESH,
        )

    def share(buf, send, recv, n, me, at):
        for d, p in enumerate(peers(n, me)):
            remote(buf.at[me], buf.at[me], send.at[d], recv.at[me], at(p)).start()

    def shared(buf, send, recv, n, me, at):
        for d, p in enumerate(peers(n, me)):
            remote(buf.at[p], buf.at[p], send.at[d], recv.at[p], at(p)).wait_recv()

    def sent(buf, send, recv, n, me, at):
        for d, p in enumerate(peers(n, me)):
            remote(buf.at[me], buf.at[me], send.at[d], recv.at[me], at(p)).wait_send()

    def tpl_copy(b):
        rows = pl.ds(b * CHUNK, CHUNK)
        return pltpu.make_async_copy(templates_hbm.at[rows], tpl.at[rows], tpl_sem.at[b])

    operands = (
        (images_hbm, images_ref),
        (tilt_hbm, tilt_ref),
        (rot_hbm, rot_ref),
        (inp_hbm, inp_ref),
        (phase_hbm, phase_ref),
        (lt_hbm, lt),
        (lq_hbm, lq),
    )
    copies = [
        pltpu.make_async_copy(src, dst, tab_sem.at[i]) for i, (src, dst) in enumerate(operands)
    ]
    copies[0].start()
    for b in range(chunks):
        tpl_copy(b).start()
    for copy in copies[1:]:
        copy.start()

    barrier = pltpu.get_barrier_semaphore()
    greeted = [at_zc(p) for p in peers(NZC, zcpos)] + [at_xy(p) for p in peers(NXY, xypos)]
    greeted += [device(chip + 1 - core, p) for p in peers(NY, ypos)]
    for target in greeted:
        pl.semaphore_signal(barrier, inc=1, device_id=target, device_id_type=MESH)

    lane = lax.broadcasted_iota(I32, (1, LANES), 1)

    copies[0].wait()
    group = group_ref[...]
    weight = jnp.zeros((1, LANES), F32)
    for g in range(NGROUP):
        weight = jnp.where(group == g, prec_ref[g], weight)
    weight = weight * (COEFS ** -0.5 * LOG2E)

    r_id = lax.broadcasted_iota(I32, (16, LANES), 0)
    l_id = lax.broadcasted_iota(I32, (16, LANES), 1)
    order_at = l_id
    for p in range(RADII):
        order_at = jnp.where(lax.div(r_id, 2) == p, l_id - ORDERS * bin_ref[p], order_at)
    order_of = [jnp.where(lax.rem(r_id, 2) == part, order_at, -1) for part in range(2)]
    select = jnp.concatenate(
        [
            jnp.concatenate([jnp.where(o == m, 1.0, 0.0).astype(BF16) for o in order_of], axis=1)
            for m in range(ORDERS)
        ],
        axis=0,
    )
    images = images_ref[...]
    img_high, img_low = split2(dot(images, select))
    shelled = jnp.concatenate([img_high, img_low], axis=0)

    def chunk_rows(b):
        return pl.ds(b * CHUNK if isinstance(b, int) else pl.multiple_of(b * CHUNK, CHUNK), CHUNK)

    def raw_stage(b):
        raw_buf[:, :LANES] = dot_t(tpl[chunk_rows(b), :], images)

    def score_stage(b):
        wide = tpl[chunk_rows(b), :].astype(F32)
        half = 0.5 * jnp.sum(wide * wide, axis=1, keepdims=True)
        score = (raw_buf[:, :LANES] - half) * weight
        score_buf[...] = score
        cmax[pl.ds(b, 1), :] = jnp.max(score, axis=0, keepdims=True)

    def exp_stage(b):
        e = jnp.exp2(score_buf[...] - cmax[pl.ds(b, 1), :])
        e_ref[chunk_rows(b), :] = e
        cmax[pl.ds(chunks + b, 1), :] = jnp.sum(e, axis=0, keepdims=True)

    waits = {0: (0,), 1: (1,), 2: (2, 3), 4: tuple(range(4, chunks))}
    for step in range(chunks + 2):
        for b in waits.get(step, ()):
            tpl_copy(b).wait()
        if step >= 2:
            exp_stage(step - 2)
        if 1 <= step <= chunks:
            score_stage(step - 1)
        if step < chunks:
            raw_stage(step)

    tops = cmax[pl.ds(0, chunks), :]
    sums = cmax[pl.ds(chunks, chunks), :]
    top = jnp.max(tops, axis=0, keepdims=True)
    total = jnp.sum(sums * jnp.exp2(tops - top), axis=0, keepdims=True)
    row8 = lax.broadcasted_iota(I32, (8, LANES), 0)
    st_buf[ypos] = jnp.where(row8 == 0, top, total)

    pl.semaphore_wait(barrier, (NZC - 1) + (NXY - 1) + (NY - 1))
    share(st_buf, st_send, st_recv, NY, ypos, at_y)

    for copy in copies[1:5]:
        copy.wait()

    angle = lax.rem(rot_ref[...] + inp_ref[...], NROT).astype(F32)
    rows_t = angle.shape[0]
    angle = jnp.concatenate([angle, jnp.zeros((LANES - rows_t, LANES), F32)], axis=0)
    angle_t[...] = angle.T.astype(BF16)

    def tilt_hot(b):
        tilt = jnp.concatenate(
            [tilt_ref[pl.ds(CUTS * b + h, 1), :] for h in range(CUTS)], axis=1
        )
        row = lax.broadcasted_iota(I32, (NTILT, CHUNK), 0)
        k_id = jnp.where(row < HALF, row, NTILT + HALF - 1 - row)
        return jnp.where(k_id == tilt, 1.0, 0.0).astype(BF16)

    row_pick = lax.broadcasted_iota(I32, (LANES, CHUNK), 0)
    lane_half = lax.div(lax.broadcasted_iota(I32, (LANES, CHUNK), 1), LANES)
    lane_turn = lax.rem(lax.broadcasted_iota(I32, (LANES, LANES), 1), NROT).astype(F32)

    def prepare_chunk(b, _):
        rows = chunk_rows(b)
        pick = jnp.where(row_pick == lane_half + CUTS * b, 1.0, 0.0).astype(BF16)
        spread = dot(angle_t[...], pick)
        hots = [
            jnp.where(spread[:, h * LANES : (h + 1) * LANES] == lane_turn, 1.0, 0.0).astype(BF16)
            for h in range(CUTS)
        ]
        ph_ref[rows, :] = dot(jnp.concatenate(hots, axis=0), phase_ref[...])
        e_high, e_low = split2(e_ref[rows, :])
        both = dot(tilt_hot(b), jnp.concatenate([e_high, e_low], axis=1))
        emass[b] = both[:, :LANES] + both[:, LANES:]
        return 0

    lax.fori_loop(0, chunks, prepare_chunk, 0)

    shared(st_buf, st_send, st_recv, NY, ypos, at_y)
    stats = [st_buf[p] for p in range(NY)]
    all_top = functools.reduce(jnp.maximum, [s[0:1] for s in stats])
    all_sum = functools.reduce(
        jnp.add, [s[1:2] * jnp.exp2(s[0:1] - all_top) for s in stats]
    )
    log_sum = jnp.log(all_sum)
    loglik_ref[...] = all_top * math.log(2.0) + log_sum
    scales = jnp.exp2((tops - all_top) - log_sum * LOG2E)
    cmax[pl.ds(0, chunks), :] = scales

    mass = jnp.zeros((NTILT, LANES), F32)
    for b in range(chunks):
        mass = mass + emass[b] * scales[b : b + 1]
    mass = jnp.broadcast_to(jnp.sum(mass, axis=1, keepdims=True), (NTILT, LANES))
    packed = jnp.zeros((8, LANES), F32)
    for q in range(4):
        for h in range(2):
            start = h * HALF + 8 * q
            packed = jnp.where(lax.div(lane, 16) == 2 * q + h, mass[start : start + 8], packed)
    m_zc[zcpos] = packed
    share(m_zc, mzc_send, mzc_recv, NZC, zcpos, at_zc)


    def weighted_stage(b):
        posterior = (e_ref[chunk_rows(b), :] * cmax[pl.ds(b, 1), :]).astype(BF16)
        raw_buf[...] = dot(jnp.concatenate([posterior, posterior], axis=1), shelled)

    def rotate_stage(b):
        rows = chunk_rows(b)
        real, imag = raw_buf[:, :LANES], raw_buf[:, LANES:]
        cosine, sine = ph_ref[rows, :LANES], ph_ref[rows, LANES:]
        for part, turned in enumerate((real * cosine + imag * sine, imag * cosine - real * sine)):
            high, low = split2(turned)
            high_buf[:, part * LANES : (part + 1) * LANES] = high
            low_buf[:, part * LANES : (part + 1) * LANES] = low

    def tilt_stage(b):
        hot = tilt_hot(b)
        return dot(hot, high_buf[...]) + dot(hot, low_buf[...])

    binned = jnp.zeros((NTILT, 2 * LANES), F32)
    for step in range(chunks + 2):
        if step >= 2:
            binned = binned + tilt_stage(step - 2)
        if 1 <= step <= chunks:
            rotate_stage(step - 1)
        if step < chunks:
            weighted_stage(step)
    bins_ref[0] = binned[:, :LANES]
    bins_ref[1] = binned[:, LANES:]

    copies[5].wait()

    sub8 = lax.broadcasted_iota(I32, (8, LANES), 0)
    lane8 = lax.broadcasted_iota(I32, (8, LANES), 1)
    even = lax.rem(sub8 + lane8, 2) == 0

    def project(k8, accs):
        accs = list(accs)
        for dk in range(8):
            k = k8 * 8 + dk
            for part in range(2):
                row = bins_ref[part, pl.ds(k, 1), :]
                mirror = bins_ref[part, pl.ds(HALF + k, 1), :]
                folded = jnp.where(even, row + mirror, row - mirror)
                for jb in range(LB):
                    accs[part * LB + jb] = (
                        accs[part * LB + jb] + lt[k, 8 * jb : 8 * jb + 8, :] * folded
                    )
        return tuple(accs)

    zero = jnp.zeros((8, LANES), F32)
    accs = lax.fori_loop(0, HALF // 8, project, (zero,) * (2 * LB))
    for q in range(2 * NYC):
        rhs_ref[q // 2, (q % 2) * 8 : (q % 2) * 8 + 8, :] = accs[q] if q < 2 * LB else zero

    r_yc[ycpos] = rhs_ref[ycpos]
    for d, p in enumerate(peers(NYC, ycpos)):
        remote(
            rhs_ref.at[p], r_yc.at[ycpos], ryc_send.at[d], ryc_recv.at[ycpos], at_yc(p)
        ).start()

    shared(m_zc, mzc_send, mzc_recv, NZC, zcpos, at_zc)
    m_xy[xypos] = functools.reduce(jnp.add, [m_zc[p] for p in range(NZC)])
    share(m_xy, mxy_send, mxy_recv, NXY, xypos, at_xy)

    copies[6].wait()
    for jb in range(LB):
        for ib in range(LB):
            if jb <= ib:
                for r in range(8 if ib < LB - 1 else 1):
                    w_ref[ib * 8 + r, 8 * jb : 8 * jb + 8, :] = (
                        jnp.where(sub8 == r, 1.0, 0.0) if ib == jb else zero
                    )

    shared(r_yc, ryc_send, ryc_recv, NYC, ycpos, at_yc)
    r_x[xpos] = functools.reduce(jnp.add, [r_yc[p] for p in range(NYC)])
    share(r_x, rx_send, rx_recv, NX, xpos, at_x)

    shared(r_x, rx_send, rx_recv, NX, xpos, at_x)
    r_z[zpos] = functools.reduce(jnp.add, [r_x[p] for p in range(NX)])
    share(r_z, rz_send, rz_recv, NZ, zpos, at_z)

    shared(m_xy, mxy_send, mxy_recv, NXY, xypos, at_xy)
    pm = functools.reduce(jnp.add, [m_xy[p] for p in range(NXY)])
    mean_mass = jnp.sum(jnp.sum(pm, axis=0, keepdims=True), axis=1, keepdims=True) / (
        16.0 * NTILT
    )
    first_half = lax.rem(lane, 32) < 16
    near = jnp.where(first_half, pm, pltpu.roll(pm, 16, 1))
    far = jnp.where(first_half, pltpu.roll(pm, LANES - 16, 1), pm)
    both_mass, diff_mass = near + far, near - far
    shell_lane = lax.div(lane, ORDERS)
    count = jnp.zeros((1, LANES), F32)
    for p in range(RADII):
        count = count + jnp.where(shell_lane == bin_ref[p], 1.0, 0.0)
    ridge = (RIDGE * mean_mass) * (count + 1.0)
    sub_even = lax.rem(sub8, 2) == 0
    for k in range(8):
        plus, minus = both_mass[k : k + 1], diff_mass[k : k + 1]
        for parity in range(2):
            signed = jnp.where(sub_even, minus, plus) if parity else jnp.where(sub_even, plus, minus)
            for jb in range(LB):
                mlq[parity * 8 + k, 8 * jb : 8 * jb + 8, :] = (
                    lq[k, 8 * jb : 8 * jb + 8, :] * signed
                )
    for ib in range(LB):

        def gram_rows(h, _, ib=ib):
            group = 4 if ib < LB - 1 else 1
            first = ib * 8 + h * 4
            acc = [[zero] * LB for _ in range(group)]
            for k in range(8):
                rows = [lq[k, pl.ds(first + r, 1), :] for r in range(group)]
                for jb in range(ib, LB):
                    for parity in range(min(group, 2)):
                        term = mlq[parity * 8 + k, 8 * jb : 8 * jb + 8, :]
                        for r in range(parity, group, 2):
                            acc[r][jb] = acc[r][jb] + term * rows[r]
            for jb in range(ib, LB):
                for r in range(group):
                    v = acc[r][jb]
                    v = v + pltpu.roll(v, 32, 1)
                    v = v + pltpu.roll(v, 64, 1)
                    v = v * count
                    if jb == ib:
                        v = v + jnp.where(sub8 == h * 4 + r, ridge, 0.0)
                    a_ref[first + r, 8 * jb : 8 * jb + 8, :] = v
            return 0

        lax.fori_loop(0, 2 if ib < LB - 1 else 1, gram_rows, 0)

    def blk(jb):
        return slice(8 * jb, 8 * jb + 8)

    for kb in range(LB):
        rows_here = 8 if kb < LB - 1 else 1
        for kk in range(rows_here):
            k = kb * 8 + kk
            rinv = 1.0 / a_ref[k, k : k + 1, :]
            dinv[k : k + 1, :] = rinv
            if k == LDEG:
                break
            upper = {jb: a_ref[k, blk(jb), :] for jb in range(kb, LB)}
            lower = {jb: w_ref[k, blk(jb), :] for jb in range(kb + 1)}
            factor = {jb: upper[jb] * rinv for jb in range(kb, LB)}
            for jb in range(kb, LB):
                pf_ref[kk, blk(jb), :] = factor[jb]
            for ii in range(kk + 1, rows_here):
                f = factor[kb][ii : ii + 1]
                for jb in range(kb, LB):
                    a_ref[kb * 8 + ii, blk(jb), :] -= f * upper[jb]
                for jb in range(kb + 1):
                    w_ref[kb * 8 + ii, blk(jb), :] -= f * lower[jb]
        for ib in range(kb + 1, LB):

            def trail(h, _, ib=ib, kb=kb):
                group = 4 if ib < LB - 1 else 1
                first = ib * 8 + h * 4
                f = [
                    [pf_ref[kk, pl.ds(first + r, 1), :] for r in range(group)] for kk in range(8)
                ]
                for ref, blocks in ((a_ref, range(ib, LB)), (w_ref, range(kb + 1))):
                    for jb in blocks:
                        v = [ref[first + r, blk(jb), :] for r in range(group)]
                        for kk in range(8):
                            u = ref[kb * 8 + kk, blk(jb), :]
                            v = [v[r] - f[kk][r] * u for r in range(group)]
                        for r in range(group):
                            ref[first + r, blk(jb), :] = v[r]
                return 0

            lax.fori_loop(0, 2 if ib < LB - 1 else 1, trail, 0)
        if kb == 0:
            shared(r_z, rz_send, rz_recv, NZ, zpos, at_z)
            r_ag[ycpos] = functools.reduce(jnp.add, [r_z[p] for p in range(NZ)])
            share(r_ag, rag_send, rag_recv, NYC, ycpos, at_yc)

    sent(st_buf, st_send, st_recv, NY, ypos, at_y)
    sent(m_zc, mzc_send, mzc_recv, NZC, zcpos, at_zc)
    sent(m_xy, mxy_send, mxy_recv, NXY, xypos, at_xy)
    for d, p in enumerate(peers(NYC, ycpos)):
        remote(
            rhs_ref.at[p], r_yc.at[ycpos], ryc_send.at[d], ryc_recv.at[ycpos], at_yc(p)
        ).wait_send()
    sent(r_x, rx_send, rx_recv, NX, xpos, at_x)
    sent(r_z, rz_send, rz_recv, NZ, zpos, at_z)
    shared(r_ag, rag_send, rag_recv, NYC, ycpos, at_yc)

    rhs = [r_ag[q // 2, (q % 2) * 8 : (q % 2) * 8 + 8, :] for q in range(2 * LB)]
    xs = (zero,) * (2 * LB)
    for ib in range(LB):

        def back(r, xs, ib=ib):
            i = ib * 8 + r
            xs = list(xs)
            rows = [w_ref[i, blk(jb), :] for jb in range(ib + 1)]
            d = dinv[pl.ds(i, 1), :]
            for part in range(2):
                t = rows[0] * rhs[part * LB]
                for jb in range(1, ib + 1):
                    t = t + rows[jb] * rhs[part * LB + jb]
                s = jnp.sum(t, axis=0, keepdims=True) * d
                for jb in range(ib + 1):
                    xs[part * LB + jb] = xs[part * LB + jb] + rows[jb] * s
            return tuple(xs)

        xs = lax.fori_loop(0, 8 if ib < LB - 1 else 1, back, xs)

    scale = math.sqrt(TEMPLATES)
    for q in range(2 * LB):
        out_ref[q // LB, blk(q % LB), :] = xs[q] * scale

    sent(r_ag, rag_send, rag_recv, NYC, ycpos, at_yc)


def arrange(x_ref, row_ref, out_ref, loglik_ref):
    loglik_ref[...] = row_ref[...]
    pad = jnp.zeros((LANES - LPAD, LANES), F32)
    for part in range(2):
        full = jnp.concatenate([x_ref[part], pad], axis=0).T
        for s in range(SHELLS):
            out_ref[:, s, part, :] = full[s * ORDERS : (s + 1) * ORDERS, :LROWS]


def body(images, templates, rotation, tilt, inplane, group, precision, radius_bin):
    t_count = templates.shape[0]
    rows = t_count // LANES
    chunks = t_count // CHUNK
    spread, packed, phases = constant_tables()
    vmem = pl.BlockSpec(memory_space=pltpu.VMEM)
    smem = pl.BlockSpec(memory_space=pltpu.SMEM)
    hbm = pl.BlockSpec(memory_space=pl.ANY)
    dma = pltpu.SemaphoreType.DMA
    solved, row = pl.pallas_call(
        kernel,
        out_shape=(
            pltpu.VMEM((2, LPAD, LANES), F32),
            pltpu.VMEM((1, LANES), F32),
        ),
        in_specs=[hbm, hbm, hbm, vmem, smem, smem, hbm, hbm, hbm, hbm, hbm],
        out_specs=(vmem, vmem),
        scratch_shapes=[
            pltpu.VMEM((rows, LANES), I32),
            pltpu.VMEM((rows, LANES), I32),
            pltpu.VMEM((rows, LANES), I32),
            pltpu.VMEM(phases.shape, BF16),
            pltpu.VMEM(images.shape, BF16),
            pltpu.VMEM((CHUNK, 2 * LANES), F32),
            pltpu.VMEM((CHUNK, LANES), F32),
            pltpu.VMEM((CHUNK, 2 * LANES), BF16),
            pltpu.VMEM((CHUNK, 2 * LANES), BF16),
            pltpu.VMEM((t_count, COEFS), BF16),
            pltpu.VMEM((HALF, LPAD, LANES), F32),
            pltpu.VMEM((8, LPAD, LANES), F32),
            pltpu.VMEM((16, LPAD, LANES), F32),
            pltpu.VMEM((t_count, LANES), F32),
            pltpu.VMEM((t_count, 2 * LANES), F32),
            pltpu.VMEM((chunks, NTILT, LANES), F32),
            pltpu.VMEM((LANES, LANES), BF16),
            pltpu.VMEM((2 * chunks, LANES), F32),
            pltpu.VMEM((LPAD, LPAD, LANES), F32),
            pltpu.VMEM((LPAD, LPAD, LANES), F32),
            pltpu.VMEM((8, LPAD, LANES), F32),
            pltpu.VMEM((LPAD, LANES), F32),
            pltpu.VMEM((2, NTILT, LANES), F32),
            pltpu.VMEM((NYC, 16, LANES), F32),
            pltpu.VMEM((NY, 8, LANES), F32),
            pltpu.VMEM((NZC, 8, LANES), F32),
            pltpu.VMEM((NXY, 8, LANES), F32),
            pltpu.VMEM((NYC, 16, LANES), F32),
            pltpu.VMEM((NX, 16, LANES), F32),
            pltpu.VMEM((NZ, 16, LANES), F32),
            pltpu.VMEM((NYC, 16, LANES), F32),
            dma((chunks,)),
            dma((7,)),
            dma((NY - 1,)),
            dma((NY,)),
            dma((NZC - 1,)),
            dma((NZC,)),
            dma((NXY - 1,)),
            dma((NXY,)),
            dma((NYC - 1,)),
            dma((NYC,)),
            dma((NX - 1,)),
            dma((NX,)),
            dma((NZ - 1,)),
            dma((NZ,)),
            dma((NYC - 1,)),
            dma((NYC,)),
        ],
        compiler_params=pltpu.CompilerParams(collective_id=0, has_side_effects=True),
        name="estep",
    )(
        tilt.reshape(rows, LANES),
        rotation.reshape(rows, LANES),
        inplane.reshape(rows, LANES),
        group.reshape(1, LANES),
        precision,
        radius_bin,
        jnp.asarray(phases),
        images,
        jnp.asarray(spread),
        jnp.asarray(packed),
        templates,
    )
    coeffs, loglik = pl.pallas_call(
        arrange,
        out_shape=(
            jax.ShapeDtypeStruct((ORDERS, SHELLS, 2, LROWS), F32),
            jax.ShapeDtypeStruct((1, LANES), F32),
        ),
        in_specs=[vmem, vmem],
        out_specs=(vmem, vmem),
        name="arrange",
    )(
        pltpu.with_memory_space_constraint(solved, pltpu.VMEM),
        pltpu.with_memory_space_constraint(row, pltpu.VMEM),
    )
    return coeffs, loglik.reshape(LANES)


def solution(mesh):
    in_specs = (
        P("img", None),
        P(("tpa", "tpb"), None),
        P(("tpa", "tpb")),
        P(("tpa", "tpb")),
        P(("tpa", "tpb")),
        P("img"),
        P(),
        P(),
    )
    out_specs = (P(), P("img"))
    return jax.shard_map(body, mesh=mesh, in_specs=in_specs, out_specs=out_specs, check_vma=False)
```

```python
import functools
import math

import jax
import jax.numpy as jnp
import numpy as np
from jax import lax
from jax.experimental import pallas as pl
from jax.experimental.pallas import tpu as pltpu
from jax.sharding import PartitionSpec as P

TEMPLATES = 16384
ORDERS = 32
RADII = 8
COEFS = 512
LDEG = 48
SHELLS = 4
NTILT = 64
NROT = 32
NGROUP = 16
RIDGE = 0.05
LOG2E = math.log2(math.e)

NX, NZ, NCORE, NY = 4, 8, 2, 4
NYC = NY * NCORE
NZC = NZ * NCORE
NXY = NX * NY
HALF = NTILT // 2
LANES = 128
LB = 7
LPAD = 8 * LB
LROWS = LDEG + 1
CHUNK = 512
CUTS = CHUNK // LANES
F32, BF16, I32 = jnp.float32, jnp.bfloat16, jnp.int32
MESH = pl.DeviceIdType.MESH


def legendre_table():
    theta = np.pi * (np.arange(NTILT) + 0.5) / NTILT
    cosine, sine = np.cos(theta)[:, None], np.sin(theta)
    orders = np.arange(ORDERS, dtype=np.float64)[None, :]
    diagonal = [np.full((NTILT,), (4.0 * np.pi) ** -0.5)]
    for m in range(1, ORDERS):
        diagonal.append(-np.sqrt((2 * m + 1) / (2.0 * m)) * sine * diagonal[-1])
    corner = np.stack(diagonal, axis=1)
    before = np.zeros((NTILT, ORDERS))
    latest = np.zeros((NTILT, ORDERS))
    columns = []
    for degree in range(LDEG + 1):
        low = float(degree - 1)
        factor = np.sqrt(
            max(4.0 * degree * degree - 1.0, 1.0)
            / np.maximum(degree * degree - orders * orders, 1.0)
        )
        factor_prev = np.sqrt(
            max(4.0 * low * low - 1.0, 1.0) / np.maximum(low * low - orders * orders, 1.0)
        )
        recurred = factor * (cosine * latest - before / factor_prev)
        current = np.where(orders == degree, corner, np.where(orders < degree, recurred, 0.0))
        columns.append(current)
        before, latest = latest, current
    return np.stack(columns, axis=2)


def constant_tables():
    legendre = legendre_table().transpose(0, 2, 1)
    padded = np.zeros((HALF, LPAD, ORDERS))
    padded[:, :LROWS] = legendre[:HALF]
    spread = np.tile(padded, (1, 1, SHELLS)).astype(np.float32)
    packed = np.concatenate([padded[q * 8 : q * 8 + 8] for q in range(4)], axis=2)
    packed = packed.astype(np.float32)
    step = np.arange(NROT)[:, None] * np.arange(ORDERS)[None, :] % NROT
    turn = 2.0 * np.pi * step / NROT
    both = np.concatenate([np.tile(np.cos(turn), (1, 4)), np.tile(np.sin(turn), (1, 4))], axis=1)
    rest, terms = both, []
    for _ in range(3):
        term = rest.astype(np.float32).astype(jnp.bfloat16)
        terms.append(term)
        rest = rest - term.astype(np.float64)
    terms.append(np.zeros_like(terms[0]))
    phases = np.concatenate(terms, axis=0)
    return spread, packed, phases


def split2(value):
    high = value.astype(BF16)
    return high, (value - high.astype(F32)).astype(BF16)


def dot(a, b):
    return lax.dot_general(a, b, (((1,), (0,)), ((), ())), preferred_element_type=F32)


def dot_t(a, b):
    return lax.dot_general(a, b, (((1,), (1,)), ((), ())), preferred_element_type=F32)


def kernel(
    tilt_hbm,
    rot_hbm,
    inp_hbm,
    group_ref,
    prec_ref,
    bin_ref,
    phase_hbm,
    images_hbm,
    lt_hbm,
    lq_hbm,
    templates_hbm,
    out_ref,
    loglik_ref,
    tilt_ref,
    rot_ref,
    inp_ref,
    phase_ref,
    images_ref,
    raw_buf,
    score_buf,
    high_buf,
    low_buf,
    tpl,
    lt,
    lq,
    mlq,
    e_ref,
    ph_ref,
    emass,
    angle_t,
    cmax,
    a_ref,
    w_ref,
    pf_ref,
    dinv,
    bins_ref,
    rhs_ref,
    st_buf,
    m_zc,
    m_xy,
    r_yc,
    r_x,
    r_z,
    r_ag,
    tpl_sem,
    tab_sem,
    st_send,
    st_recv,
    mzc_send,
    mzc_recv,
    mxy_send,
    mxy_recv,
    ryc_send,
    ryc_recv,
    rx_send,
    rx_recv,
    rz_send,
    rz_recv,
    rag_send,
    rag_recv,
):
    t_count = templates_hbm.shape[0]
    chunks = t_count // CHUNK
    img = lax.axis_index("img")
    tpa = lax.axis_index("tpa")
    tpb = lax.axis_index("tpb")
    core = lax.rem(img, NCORE)
    zpos = lax.rem(lax.div(img, NCORE), NZ)
    xpos = lax.div(img, NCORE * NZ)
    ypos = tpa * 2 + tpb
    ycpos = core * NY + ypos

    zcpos = zpos * NCORE + core
    xypos = xpos * NY + ypos
    chip = img - core
    column = img - zcpos

    def device(at_img, y):
        return {"img": at_img, "tpa": lax.div(y, 2), "tpb": lax.rem(y, 2)}

    def at_y(p):
        return device(img, p)

    def at_yc(p):
        return device(chip + lax.div(p, NY), lax.rem(p, NY))

    def at_x(p):
        return {"img": p * NZC + zcpos, "tpa": tpa, "tpb": tpb}

    def at_z(p):
        return {"img": column + p * NCORE + core, "tpa": tpa, "tpb": tpb}

    def at_zc(p):
        return {"img": column + p, "tpa": tpa, "tpb": tpb}

    def at_xy(p):
        return device(lax.div(p, NY) * NZC + zcpos, lax.rem(p, NY))

    def peers(n, me):
        return [lax.rem(me + d, n) for d in range(1, n)]

    def remote(src, dst, send, recv, device):
        return pltpu.make_async_remote_copy(
            src_ref=src,
            dst_ref=dst,
            send_sem=send,
            recv_sem=recv,
            device_id=device,
            device_id_type=MESH,
        )

    def share(buf, send, recv, n, me, at):
        for d, p in enumerate(peers(n, me)):
            remote(buf.at[me], buf.at[me], send.at[d], recv.at[me], at(p)).start()

    def shared(buf, send, recv, n, me, at):
        for d, p in enumerate(peers(n, me)):
            remote(buf.at[p], buf.at[p], send.at[d], recv.at[p], at(p)).wait_recv()

    def sent(buf, send, recv, n, me, at):
        for d, p in enumerate(peers(n, me)):
            remote(buf.at[me], buf.at[me], send.at[d], recv.at[me], at(p)).wait_send()

    def tpl_copy(b):
        rows = pl.ds(b * CHUNK, CHUNK)
        return pltpu.make_async_copy(templates_hbm.at[rows], tpl.at[rows], tpl_sem.at[b])

    operands = (
        (images_hbm, images_ref),
        (tilt_hbm, tilt_ref),
        (rot_hbm, rot_ref),
        (inp_hbm, inp_ref),
        (phase_hbm, phase_ref),
        (lt_hbm, lt),
        (lq_hbm, lq),
    )
    copies = [
        pltpu.make_async_copy(src, dst, tab_sem.at[i]) for i, (src, dst) in enumerate(operands)
    ]
    copies[0].start()
    for b in range(chunks):
        tpl_copy(b).start()
    for copy in copies[1:]:
        copy.start()

    barrier = pltpu.get_barrier_semaphore()
    greeted = [at_zc(p) for p in peers(NZC, zcpos)] + [at_xy(p) for p in peers(NXY, xypos)]
    greeted += [device(chip + 1 - core, p) for p in peers(NY, ypos)]
    for target in greeted:
        pl.semaphore_signal(barrier, inc=1, device_id=target, device_id_type=MESH)

    lane = lax.broadcasted_iota(I32, (1, LANES), 1)

    copies[0].wait()
    group = group_ref[...]
    weight = jnp.zeros((1, LANES), F32)
    for g in range(NGROUP):
        weight = jnp.where(group == g, prec_ref[g], weight)
    weight = weight * (COEFS ** -0.5 * LOG2E)

    r_id = lax.broadcasted_iota(I32, (16, LANES), 0)
    l_id = lax.broadcasted_iota(I32, (16, LANES), 1)
    order_at = l_id
    for p in range(RADII):
        order_at = jnp.where(lax.div(r_id, 2) == p, l_id - ORDERS * bin_ref[p], order_at)
    order_of = [jnp.where(lax.rem(r_id, 2) == part, order_at, -1) for part in range(2)]
    select = jnp.concatenate(
        [
            jnp.concatenate([jnp.where(o == m, 1.0, 0.0).astype(BF16) for o in order_of], axis=1)
            for m in range(ORDERS)
        ],
        axis=0,
    )
    images = images_ref[...]
    img_high, img_low = split2(dot(images, select))
    shelled = jnp.concatenate([img_high, img_low], axis=0)

    def chunk_rows(b):
        return pl.ds(b * CHUNK if isinstance(b, int) else pl.multiple_of(b * CHUNK, CHUNK), CHUNK)

    def raw_stage(b):
        raw_buf[:, :LANES] = dot_t(tpl[chunk_rows(b), :], images)

    def score_stage(b):
        wide = tpl[chunk_rows(b), :].astype(F32)
        half = 0.5 * jnp.sum(wide * wide, axis=1, keepdims=True)
        score = (raw_buf[:, :LANES] - half) * weight
        score_buf[...] = score
        cmax[pl.ds(b, 1), :] = jnp.max(score, axis=0, keepdims=True)

    def exp_stage(b):
        e = jnp.exp2(score_buf[...] - cmax[pl.ds(b, 1), :])
        e_ref[chunk_rows(b), :] = e
        cmax[pl.ds(chunks + b, 1), :] = jnp.sum(e, axis=0, keepdims=True)

    waits = {0: (0,), 1: (1,), 2: (2, 3), 4: tuple(range(4, chunks))}
    for step in range(chunks + 2):
        for b in waits.get(step, ()):
            tpl_copy(b).wait()
        if step >= 2:
            exp_stage(step - 2)
        if 1 <= step <= chunks:
            score_stage(step - 1)
        if step < chunks:
            raw_stage(step)

    tops = cmax[pl.ds(0, chunks), :]
    sums = cmax[pl.ds(chunks, chunks), :]
    top = jnp.max(tops, axis=0, keepdims=True)
    total = jnp.sum(sums * jnp.exp2(tops - top), axis=0, keepdims=True)
    row8 = lax.broadcasted_iota(I32, (8, LANES), 0)
    st_buf[ypos] = jnp.where(row8 == 0, top, total)

    pl.semaphore_wait(barrier, (NZC - 1) + (NXY - 1) + (NY - 1))
    share(st_buf, st_send, st_recv, NY, ypos, at_y)

    for copy in copies[1:5]:
        copy.wait()

    angle = lax.rem(rot_ref[...] + inp_ref[...], NROT).astype(F32)
    rows_t = angle.shape[0]
    angle = jnp.concatenate([angle, jnp.zeros((LANES - rows_t, LANES), F32)], axis=0)
    angle_t[...] = angle.T.astype(BF16)

    def tilt_hot(b):
        tilt = jnp.concatenate(
            [tilt_ref[pl.ds(CUTS * b + h, 1), :] for h in range(CUTS)], axis=1
        )
        row = lax.broadcasted_iota(I32, (NTILT, CHUNK), 0)
        k_id = jnp.where(row < HALF, row, NTILT + HALF - 1 - row)
        return jnp.where(k_id == tilt, 1.0, 0.0).astype(BF16)

    row_pick = lax.broadcasted_iota(I32, (LANES, CHUNK), 0)
    lane_half = lax.div(lax.broadcasted_iota(I32, (LANES, CHUNK), 1), LANES)
    lane_turn = lax.rem(lax.broadcasted_iota(I32, (LANES, LANES), 1), NROT).astype(F32)

    def prepare_chunk(b, _):
        rows = chunk_rows(b)
        pick = jnp.where(row_pick == lane_half + CUTS * b, 1.0, 0.0).astype(BF16)
        spread = dot(angle_t[...], pick)
        hots = [
            jnp.where(spread[:, h * LANES : (h + 1) * LANES] == lane_turn, 1.0, 0.0).astype(BF16)
            for h in range(CUTS)
        ]
        ph_ref[rows, :] = dot(jnp.concatenate(hots, axis=0), phase_ref[...])
        e_high, e_low = split2(e_ref[rows, :])
        both = dot(tilt_hot(b), jnp.concatenate([e_high, e_low], axis=1))
        emass[b] = both[:, :LANES] + both[:, LANES:]
        return 0

    lax.fori_loop(0, chunks, prepare_chunk, 0)

    shared(st_buf, st_send, st_recv, NY, ypos, at_y)
    stats = [st_buf[p] for p in range(NY)]
    all_top = functools.reduce(jnp.maximum, [s[0:1] for s in stats])
    all_sum = functools.reduce(
        jnp.add, [s[1:2] * jnp.exp2(s[0:1] - all_top) for s in stats]
    )
    log_sum = jnp.log(all_sum)
    loglik_ref[...] = all_top * math.log(2.0) + log_sum
    scales = jnp.exp2((tops - all_top) - log_sum * LOG2E)
    cmax[pl.ds(0, chunks), :] = scales


    def weighted_stage(b):
        posterior = (e_ref[chunk_rows(b), :] * cmax[pl.ds(b, 1), :]).astype(BF16)
        raw_buf[...] = dot(jnp.concatenate([posterior, posterior], axis=1), shelled)

    def rotate_stage(b):
        rows = chunk_rows(b)
        real, imag = raw_buf[:, :LANES], raw_buf[:, LANES:]
        cosine, sine = ph_ref[rows, :LANES], ph_ref[rows, LANES:]
        for part, turned in enumerate((real * cosine + imag * sine, imag * cosine - real * sine)):
            high, low = split2(turned)
            high_buf[:, part * LANES : (part + 1) * LANES] = high
            low_buf[:, part * LANES : (part + 1) * LANES] = low

    def tilt_stage(b):
        hot = tilt_hot(b)
        return dot(hot, high_buf[...]) + dot(hot, low_buf[...])

    binned = jnp.zeros((NTILT, 2 * LANES), F32)
    for step in range(chunks + 2):
        if step >= 2:
            binned = binned + tilt_stage(step - 2)
        if 1 <= step <= chunks:
            rotate_stage(step - 1)
        if step < chunks:
            weighted_stage(step)
    bins_ref[0] = binned[:, :LANES]
    bins_ref[1] = binned[:, LANES:]

    copies[5].wait()

    sub8 = lax.broadcasted_iota(I32, (8, LANES), 0)
    lane8 = lax.broadcasted_iota(I32, (8, LANES), 1)
    even = lax.rem(sub8 + lane8, 2) == 0

    def project(k8, accs):
        accs = list(accs)
        for dk in range(8):
            k = k8 * 8 + dk
            for part in range(2):
                row = bins_ref[part, pl.ds(k, 1), :]
                mirror = bins_ref[part, pl.ds(HALF + k, 1), :]
                folded = jnp.where(even, row + mirror, row - mirror)
                for jb in range(LB):
                    accs[part * LB + jb] = (
                        accs[part * LB + jb] + lt[k, 8 * jb : 8 * jb + 8, :] * folded
                    )
        return tuple(accs)

    zero = jnp.zeros((8, LANES), F32)
    accs = lax.fori_loop(0, HALF // 8, project, (zero,) * (2 * LB))
    for q in range(2 * NYC):
        rhs_ref[q // 2, (q % 2) * 8 : (q % 2) * 8 + 8, :] = accs[q] if q < 2 * LB else zero

    r_yc[ycpos] = rhs_ref[ycpos]
    for d, p in enumerate(peers(NYC, ycpos)):
        remote(
            rhs_ref.at[p], r_yc.at[ycpos], ryc_send.at[d], ryc_recv.at[ycpos], at_yc(p)
        ).start()

    mass = jnp.zeros((NTILT, LANES), F32)
    for b in range(chunks):
        mass = mass + emass[b] * scales[b : b + 1]
    mass = jnp.broadcast_to(jnp.sum(mass, axis=1, keepdims=True), (NTILT, LANES))
    packed = jnp.zeros((8, LANES), F32)
    for q in range(4):
        for h in range(2):
            start = h * HALF + 8 * q
            packed = jnp.where(lax.div(lane, 16) == 2 * q + h, mass[start : start + 8], packed)
    m_zc[zcpos] = packed
    share(m_zc, mzc_send, mzc_recv, NZC, zcpos, at_zc)

    copies[6].wait()
    for jb in range(LB):
        for ib in range(LB):
            if jb <= ib:
                for r in range(8 if ib < LB - 1 else 1):
                    w_ref[ib * 8 + r, 8 * jb : 8 * jb + 8, :] = (
                        jnp.where(sub8 == r, 1.0, 0.0) if ib == jb else zero
                    )

    shared(r_yc, ryc_send, ryc_recv, NYC, ycpos, at_yc)
    r_x[xpos] = functools.reduce(jnp.add, [r_yc[p] for p in range(NYC)])
    share(r_x, rx_send, rx_recv, NX, xpos, at_x)

    shared(m_zc, mzc_send, mzc_recv, NZC, zcpos, at_zc)
    m_xy[xypos] = functools.reduce(jnp.add, [m_zc[p] for p in range(NZC)])
    share(m_xy, mxy_send, mxy_recv, NXY, xypos, at_xy)

    shared(r_x, rx_send, rx_recv, NX, xpos, at_x)
    r_z[zpos] = functools.reduce(jnp.add, [r_x[p] for p in range(NX)])
    share(r_z, rz_send, rz_recv, NZ, zpos, at_z)

    shared(m_xy, mxy_send, mxy_recv, NXY, xypos, at_xy)
    pm = functools.reduce(jnp.add, [m_xy[p] for p in range(NXY)])
    mean_mass = jnp.sum(jnp.sum(pm, axis=0, keepdims=True), axis=1, keepdims=True) / (
        16.0 * NTILT
    )
    first_half = lax.rem(lane, 32) < 16
    near = jnp.where(first_half, pm, pltpu.roll(pm, 16, 1))
    far = jnp.where(first_half, pltpu.roll(pm, LANES - 16, 1), pm)
    both_mass, diff_mass = near + far, near - far
    shell_lane = lax.div(lane, ORDERS)
    count = jnp.zeros((1, LANES), F32)
    for p in range(RADII):
        count = count + jnp.where(shell_lane == bin_ref[p], 1.0, 0.0)
    ridge = (RIDGE * mean_mass) * (count + 1.0)
    sub_even = lax.rem(sub8, 2) == 0
    for k in range(8):
        plus, minus = both_mass[k : k + 1], diff_mass[k : k + 1]
        for parity in range(2):
            signed = jnp.where(sub_even, minus, plus) if parity else jnp.where(sub_even, plus, minus)
            for jb in range(LB):
                mlq[parity * 8 + k, 8 * jb : 8 * jb + 8, :] = (
                    lq[k, 8 * jb : 8 * jb + 8, :] * signed
                )
    for ib in range(LB):

        def gram_rows(h, _, ib=ib):
            group = 4 if ib < LB - 1 else 1
            first = ib * 8 + h * 4
            acc = [[zero] * LB for _ in range(group)]
            for k in range(8):
                rows = [lq[k, pl.ds(first + r, 1), :] for r in range(group)]
                for jb in range(ib, LB):
                    for parity in range(min(group, 2)):
                        term = mlq[parity * 8 + k, 8 * jb : 8 * jb + 8, :]
                        for r in range(parity, group, 2):
                            acc[r][jb] = acc[r][jb] + term * rows[r]
            for jb in range(ib, LB):
                for r in range(group):
                    v = acc[r][jb]
                    v = v + pltpu.roll(v, 32, 1)
                    v = v + pltpu.roll(v, 64, 1)
                    v = v * count
                    if jb == ib:
                        v = v + jnp.where(sub8 == h * 4 + r, ridge, 0.0)
                    a_ref[first + r, 8 * jb : 8 * jb + 8, :] = v
            return 0

        lax.fori_loop(0, 2 if ib < LB - 1 else 1, gram_rows, 0)

    shared(r_z, rz_send, rz_recv, NZ, zpos, at_z)
    r_ag[ycpos] = functools.reduce(jnp.add, [r_z[p] for p in range(NZ)])
    share(r_ag, rag_send, rag_recv, NYC, ycpos, at_yc)

    def blk(jb):
        return slice(8 * jb, 8 * jb + 8)

    for kb in range(LB):
        rows_here = 8 if kb < LB - 1 else 1
        for kk in range(rows_here):
            k = kb * 8 + kk
            rinv = 1.0 / a_ref[k, k : k + 1, :]
            dinv[k : k + 1, :] = rinv
            if k == LDEG:
                break
            upper = {jb: a_ref[k, blk(jb), :] for jb in range(kb, LB)}
            lower = {jb: w_ref[k, blk(jb), :] for jb in range(kb + 1)}
            factor = {jb: upper[jb] * rinv for jb in range(kb, LB)}
            for jb in range(kb, LB):
                pf_ref[kk, blk(jb), :] = factor[jb]
            for ii in range(kk + 1, rows_here):
                f = factor[kb][ii : ii + 1]
                for jb in range(kb, LB):
                    a_ref[kb * 8 + ii, blk(jb), :] -= f * upper[jb]
                for jb in range(kb + 1):
                    w_ref[kb * 8 + ii, blk(jb), :] -= f * lower[jb]
        for ib in range(kb + 1, LB):

            def trail(h, _, ib=ib, kb=kb):
                group = 4 if ib < LB - 1 else 1
                first = ib * 8 + h * 4
                f = [
                    [pf_ref[kk, pl.ds(first + r, 1), :] for r in range(group)] for kk in range(8)
                ]
                for ref, blocks in ((a_ref, range(ib, LB)), (w_ref, range(kb + 1))):
                    for jb in blocks:
                        v = [ref[first + r, blk(jb), :] for r in range(group)]
                        for kk in range(8):
                            u = ref[kb * 8 + kk, blk(jb), :]
                            v = [v[r] - f[kk][r] * u for r in range(group)]
                        for r in range(group):
                            ref[first + r, blk(jb), :] = v[r]
                return 0

            lax.fori_loop(0, 2 if ib < LB - 1 else 1, trail, 0)

    sent(st_buf, st_send, st_recv, NY, ypos, at_y)
    sent(m_zc, mzc_send, mzc_recv, NZC, zcpos, at_zc)
    sent(m_xy, mxy_send, mxy_recv, NXY, xypos, at_xy)
    for d, p in enumerate(peers(NYC, ycpos)):
        remote(
            rhs_ref.at[p], r_yc.at[ycpos], ryc_send.at[d], ryc_recv.at[ycpos], at_yc(p)
        ).wait_send()
    sent(r_x, rx_send, rx_recv, NX, xpos, at_x)
    sent(r_z, rz_send, rz_recv, NZ, zpos, at_z)
    shared(r_ag, rag_send, rag_recv, NYC, ycpos, at_yc)

    rhs = [r_ag[q // 2, (q % 2) * 8 : (q % 2) * 8 + 8, :] for q in range(2 * LB)]
    xs = [zero] * (2 * LB)
    for i in range(LROWS):
        ib = i // 8
        rows = [w_ref[i, blk(jb), :] for jb in range(ib + 1)]
        for part in range(2):
            t = rows[0] * rhs[part * LB]
            for jb in range(1, ib + 1):
                t = t + rows[jb] * rhs[part * LB + jb]
            s = jnp.sum(t, axis=0, keepdims=True) * dinv[i : i + 1, :]
            for jb in range(ib + 1):
                xs[part * LB + jb] = xs[part * LB + jb] + rows[jb] * s

    scale = math.sqrt(TEMPLATES)
    for q in range(2 * LB):
        out_ref[q // LB, blk(q % LB), :] = xs[q] * scale

    sent(r_ag, rag_send, rag_recv, NYC, ycpos, at_yc)


def arrange(x_ref, row_ref, out_ref, loglik_ref):
    loglik_ref[...] = row_ref[...]
    pad = jnp.zeros((LANES - LPAD, LANES), F32)
    for part in range(2):
        full = jnp.concatenate([x_ref[part], pad], axis=0).T
        for s in range(SHELLS):
            out_ref[:, s, part, :] = full[s * ORDERS : (s + 1) * ORDERS, :LROWS]


def body(images, templates, rotation, tilt, inplane, group, precision, radius_bin):
    t_count = templates.shape[0]
    rows = t_count // LANES
    chunks = t_count // CHUNK
    spread, packed, phases = constant_tables()
    vmem = pl.BlockSpec(memory_space=pltpu.VMEM)
    smem = pl.BlockSpec(memory_space=pltpu.SMEM)
    hbm = pl.BlockSpec(memory_space=pl.ANY)
    dma = pltpu.SemaphoreType.DMA
    solved, row = pl.pallas_call(
        kernel,
        out_shape=(
            pltpu.VMEM((2, LPAD, LANES), F32),
            pltpu.VMEM((1, LANES), F32),
        ),
        in_specs=[hbm, hbm, hbm, vmem, smem, smem, hbm, hbm, hbm, hbm, hbm],
        out_specs=(vmem, vmem),
        scratch_shapes=[
            pltpu.VMEM((rows, LANES), I32),
            pltpu.VMEM((rows, LANES), I32),
            pltpu.VMEM((rows, LANES), I32),
            pltpu.VMEM(phases.shape, BF16),
            pltpu.VMEM(images.shape, BF16),
            pltpu.VMEM((CHUNK, 2 * LANES), F32),
            pltpu.VMEM((CHUNK, LANES), F32),
            pltpu.VMEM((CHUNK, 2 * LANES), BF16),
            pltpu.VMEM((CHUNK, 2 * LANES), BF16),
            pltpu.VMEM((t_count, COEFS), BF16),
            pltpu.VMEM((HALF, LPAD, LANES), F32),
            pltpu.VMEM((8, LPAD, LANES), F32),
            pltpu.VMEM((16, LPAD, LANES), F32),
            pltpu.VMEM((t_count, LANES), F32),
            pltpu.VMEM((t_count, 2 * LANES), F32),
            pltpu.VMEM((chunks, NTILT, LANES), F32),
            pltpu.VMEM((LANES, LANES), BF16),
            pltpu.VMEM((2 * chunks, LANES), F32),
            pltpu.VMEM((LPAD, LPAD, LANES), F32),
            pltpu.VMEM((LPAD, LPAD, LANES), F32),
            pltpu.VMEM((8, LPAD, LANES), F32),
            pltpu.VMEM((LPAD, LANES), F32),
            pltpu.VMEM((2, NTILT, LANES), F32),
            pltpu.VMEM((NYC, 16, LANES), F32),
            pltpu.VMEM((NY, 8, LANES), F32),
            pltpu.VMEM((NZC, 8, LANES), F32),
            pltpu.VMEM((NXY, 8, LANES), F32),
            pltpu.VMEM((NYC, 16, LANES), F32),
            pltpu.VMEM((NX, 16, LANES), F32),
            pltpu.VMEM((NZ, 16, LANES), F32),
            pltpu.VMEM((NYC, 16, LANES), F32),
            dma((chunks,)),
            dma((7,)),
            dma((NY - 1,)),
            dma((NY,)),
            dma((NZC - 1,)),
            dma((NZC,)),
            dma((NXY - 1,)),
            dma((NXY,)),
            dma((NYC - 1,)),
            dma((NYC,)),
            dma((NX - 1,)),
            dma((NX,)),
            dma((NZ - 1,)),
            dma((NZ,)),
            dma((NYC - 1,)),
            dma((NYC,)),
        ],
        compiler_params=pltpu.CompilerParams(collective_id=0, has_side_effects=True),
        name="estep",
    )(
        tilt.reshape(rows, LANES),
        rotation.reshape(rows, LANES),
        inplane.reshape(rows, LANES),
        group.reshape(1, LANES),
        precision,
        radius_bin,
        jnp.asarray(phases),
        images,
        jnp.asarray(spread),
        jnp.asarray(packed),
        templates,
    )
    coeffs, loglik = pl.pallas_call(
        arrange,
        out_shape=(
            jax.ShapeDtypeStruct((ORDERS, SHELLS, 2, LROWS), F32),
            jax.ShapeDtypeStruct((1, LANES), F32),
        ),
        in_specs=[vmem, vmem],
        out_specs=(vmem, vmem),
        name="arrange",
    )(
        pltpu.with_memory_space_constraint(solved, pltpu.VMEM),
        pltpu.with_memory_space_constraint(row, pltpu.VMEM),
    )
    return coeffs, loglik.reshape(LANES)


def solution(mesh):
    in_specs = (
        P("img", None),
        P(("tpa", "tpb"), None),
        P(("tpa", "tpb")),
        P(("tpa", "tpb")),
        P(("tpa", "tpb")),
        P("img"),
        P(),
        P(),
    )
    out_specs = (P(), P("img"))
    return jax.shard_map(body, mesh=mesh, in_specs=in_specs, out_specs=out_specs, check_vma=False)
```

```python
import functools
import math

import jax
import jax.numpy as jnp
import numpy as np
from jax import lax
from jax.experimental import pallas as pl
from jax.experimental.pallas import tpu as pltpu
from jax.sharding import PartitionSpec as P

TEMPLATES = 16384
ORDERS = 32
RADII = 8
COEFS = 512
LDEG = 48
SHELLS = 4
NTILT = 64
NROT = 32
NGROUP = 16
RIDGE = 0.05
LOG2E = math.log2(math.e)

NX, NZ, NCORE, NY = 4, 8, 2, 4
NYC = NY * NCORE
NZC = NZ * NCORE
NXY = NX * NY
HALF = NTILT // 2
LANES = 128
LB = 7
LPAD = 8 * LB
LROWS = LDEG + 1
CHUNK = 512
CUTS = CHUNK // LANES
F32, BF16, I32 = jnp.float32, jnp.bfloat16, jnp.int32
MESH = pl.DeviceIdType.MESH


def legendre_table():
    theta = np.pi * (np.arange(NTILT) + 0.5) / NTILT
    cosine, sine = np.cos(theta)[:, None], np.sin(theta)
    orders = np.arange(ORDERS, dtype=np.float64)[None, :]
    diagonal = [np.full((NTILT,), (4.0 * np.pi) ** -0.5)]
    for m in range(1, ORDERS):
        diagonal.append(-np.sqrt((2 * m + 1) / (2.0 * m)) * sine * diagonal[-1])
    corner = np.stack(diagonal, axis=1)
    before = np.zeros((NTILT, ORDERS))
    latest = np.zeros((NTILT, ORDERS))
    columns = []
    for degree in range(LDEG + 1):
        low = float(degree - 1)
        factor = np.sqrt(
            max(4.0 * degree * degree - 1.0, 1.0)
            / np.maximum(degree * degree - orders * orders, 1.0)
        )
        factor_prev = np.sqrt(
            max(4.0 * low * low - 1.0, 1.0) / np.maximum(low * low - orders * orders, 1.0)
        )
        recurred = factor * (cosine * latest - before / factor_prev)
        current = np.where(orders == degree, corner, np.where(orders < degree, recurred, 0.0))
        columns.append(current)
        before, latest = latest, current
    return np.stack(columns, axis=2)


def constant_tables():
    legendre = legendre_table().transpose(0, 2, 1)
    padded = np.zeros((HALF, LPAD, ORDERS))
    padded[:, :LROWS] = legendre[:HALF]
    spread = np.tile(padded, (1, 1, SHELLS)).astype(np.float32)
    packed = np.concatenate([padded[q * 8 : q * 8 + 8] for q in range(4)], axis=2)
    packed = packed.astype(np.float32)
    step = np.arange(NROT)[:, None] * np.arange(ORDERS)[None, :] % NROT
    turn = 2.0 * np.pi * step / NROT
    both = np.concatenate([np.tile(np.cos(turn), (1, 4)), np.tile(np.sin(turn), (1, 4))], axis=1)
    rest, terms = both, []
    for _ in range(3):
        term = rest.astype(np.float32).astype(jnp.bfloat16)
        terms.append(term)
        rest = rest - term.astype(np.float64)
    terms.append(np.zeros_like(terms[0]))
    phases = np.concatenate(terms, axis=0)
    return spread, packed, phases


def split2(value):
    high = value.astype(BF16)
    return high, (value - high.astype(F32)).astype(BF16)


def dot(a, b):
    return lax.dot_general(a, b, (((1,), (0,)), ((), ())), preferred_element_type=F32)


def dot_t(a, b):
    return lax.dot_general(a, b, (((1,), (1,)), ((), ())), preferred_element_type=F32)


def kernel(
    tilt_hbm,
    rot_hbm,
    inp_hbm,
    group_hbm,
    prec_hbm,
    radius_hbm,
    phase_hbm,
    images_hbm,
    lt_hbm,
    lq_hbm,
    templates_hbm,
    out_ref,
    loglik_ref,
    tilt_ref,
    rot_ref,
    inp_ref,
    group_ref,
    prec_ref,
    radius_ref,
    phase_ref,
    images_ref,
    raw_buf,
    score_buf,
    high_buf,
    low_buf,
    tpl,
    lt,
    lq,
    mlq,
    e_ref,
    ph_ref,
    emass,
    angle_t,
    cmax,
    a_ref,
    w_ref,
    pf_ref,
    dinv,
    bins_ref,
    rhs_ref,
    st_buf,
    m_zc,
    m_xy,
    r_yc,
    r_x,
    r_z,
    r_ag,
    tpl_sem,
    tab_sem,
    st_send,
    st_recv,
    mzc_send,
    mzc_recv,
    mxy_send,
    mxy_recv,
    ryc_send,
    ryc_recv,
    rx_send,
    rx_recv,
    rz_send,
    rz_recv,
    rag_send,
    rag_recv,
):
    t_count = templates_hbm.shape[0]
    chunks = t_count // CHUNK
    img = lax.axis_index("img")
    tpa = lax.axis_index("tpa")
    tpb = lax.axis_index("tpb")
    core = lax.rem(img, NCORE)
    zpos = lax.rem(lax.div(img, NCORE), NZ)
    xpos = lax.div(img, NCORE * NZ)
    ypos = tpb * 2 + tpa
    ycpos = core * NY + ypos

    zcpos = zpos * NCORE + core
    xypos = xpos * NY + ypos
    chip = img - core
    column = img - zcpos

    def device(at_img, y):
        return {"img": at_img, "tpa": lax.rem(y, 2), "tpb": lax.div(y, 2)}

    def at_y(p):
        return device(img, p)

    def at_yc(p):
        return device(chip + lax.div(p, NY), lax.rem(p, NY))

    def at_x(p):
        return {"img": p * NZC + zcpos, "tpa": tpa, "tpb": tpb}

    def at_z(p):
        return {"img": column + p * NCORE + core, "tpa": tpa, "tpb": tpb}

    def at_zc(p):
        return {"img": column + p, "tpa": tpa, "tpb": tpb}

    def at_xy(p):
        return device(lax.div(p, NY) * NZC + zcpos, lax.rem(p, NY))

    def peers(n, me):
        if n == NYC and me is ycpos:
            steps = (2, 6, 1, 3, 5, 7, 4)
        else:
            steps = sorted(range(1, n), key=lambda d: -min(d, n - d))
        return [lax.rem(me + d, n) for d in steps]

    def remote(src, dst, send, recv, device):
        return pltpu.make_async_remote_copy(
            src_ref=src,
            dst_ref=dst,
            send_sem=send,
            recv_sem=recv,
            device_id=device,
            device_id_type=MESH,
        )

    def share(buf, send, recv, n, me, at):
        for d, p in enumerate(peers(n, me)):
            remote(buf.at[me], buf.at[me], send.at[d], recv.at[me], at(p)).start()

    def shared(buf, send, recv, n, me, at):
        for d, p in enumerate(peers(n, me)):
            remote(buf.at[p], buf.at[p], send.at[d], recv.at[p], at(p)).wait_recv()

    def sent(buf, send, recv, n, me, at):
        for d, p in enumerate(peers(n, me)):
            remote(buf.at[me], buf.at[me], send.at[d], recv.at[me], at(p)).wait_send()

    def tpl_copy(b):
        rows = pl.ds(b * CHUNK, CHUNK)
        return pltpu.make_async_copy(templates_hbm.at[rows], tpl.at[rows], tpl_sem.at[b])

    operands = (
        (images_hbm, images_ref),
        (tilt_hbm, tilt_ref),
        (rot_hbm, rot_ref),
        (inp_hbm, inp_ref),
        (phase_hbm, phase_ref),
        (lt_hbm, lt),
        (lq_hbm, lq),
        (group_hbm, group_ref),
        (prec_hbm, prec_ref),
        (radius_hbm, radius_ref),
    )
    copies = [
        pltpu.make_async_copy(src, dst, tab_sem.at[i]) for i, (src, dst) in enumerate(operands)
    ]
    for i in (7, 8, 9, 0):
        copies[i].start()
    for b in range(chunks):
        tpl_copy(b).start()
    for copy in copies[1:7]:
        copy.start()

    barrier = pltpu.get_barrier_semaphore()
    greeted = [at_zc(p) for p in peers(NZC, zcpos)] + [at_xy(p) for p in peers(NXY, xypos)]
    greeted += [device(chip + 1 - core, p) for p in peers(NY, ypos)]
    for target in greeted:
        pl.semaphore_signal(barrier, inc=1, device_id=target, device_id_type=MESH)

    lane = lax.broadcasted_iota(I32, (1, LANES), 1)

    for i in (7, 8, 9, 0):
        copies[i].wait()
    group = group_ref[...]
    weight = jnp.zeros((1, LANES), F32)
    for g in range(NGROUP):
        weight = jnp.where(group == g, prec_ref[:, g : g + 1], weight)
    weight = weight * (COEFS ** -0.5 * LOG2E)

    r_id = lax.broadcasted_iota(I32, (16, LANES), 0)
    l_id = lax.broadcasted_iota(I32, (16, LANES), 1)
    order_at = l_id
    for p in range(RADII):
        order_at = jnp.where(lax.div(r_id, 2) == p, l_id - ORDERS * radius_ref[:, p : p + 1], order_at)
    order_of = [jnp.where(lax.rem(r_id, 2) == part, order_at, -1) for part in range(2)]
    select = jnp.concatenate(
        [
            jnp.concatenate([jnp.where(o == m, 1.0, 0.0).astype(BF16) for o in order_of], axis=1)
            for m in range(ORDERS)
        ],
        axis=0,
    )
    images = images_ref[...]
    img_high, img_low = split2(dot(images, select))
    shelled = jnp.concatenate([img_high, img_low], axis=0)

    def chunk_rows(b):
        return pl.ds(b * CHUNK if isinstance(b, int) else pl.multiple_of(b * CHUNK, CHUNK), CHUNK)

    def raw_stage(b):
        raw_buf[:, :LANES] = dot_t(tpl[chunk_rows(b), :], images)

    def score_stage(b):
        wide = tpl[chunk_rows(b), :].astype(F32)
        half = 0.5 * jnp.sum(wide * wide, axis=1, keepdims=True)
        score = (raw_buf[:, :LANES] - half) * weight
        score_buf[...] = score
        cmax[pl.ds(b, 1), :] = jnp.max(score, axis=0, keepdims=True)

    def exp_stage(b):
        e = jnp.exp2(score_buf[...] - cmax[pl.ds(b, 1), :])
        e_ref[chunk_rows(b), :] = e
        cmax[pl.ds(chunks + b, 1), :] = jnp.sum(e, axis=0, keepdims=True)

    waits = {0: (0,), 1: (1,), 2: (2, 3), 4: tuple(range(4, chunks))}
    for step in range(chunks + 2):
        for b in waits.get(step, ()):
            tpl_copy(b).wait()
        if step >= 2:
            exp_stage(step - 2)
        if 1 <= step <= chunks:
            score_stage(step - 1)
        if step < chunks:
            raw_stage(step)

    tops = cmax[pl.ds(0, chunks), :]
    sums = cmax[pl.ds(chunks, chunks), :]
    top = jnp.max(tops, axis=0, keepdims=True)
    total = jnp.sum(sums * jnp.exp2(tops - top), axis=0, keepdims=True)
    row8 = lax.broadcasted_iota(I32, (8, LANES), 0)
    st_buf[ypos] = jnp.where(row8 == 0, top, total)

    pl.semaphore_wait(barrier, (NZC - 1) + (NXY - 1) + (NY - 1))
    share(st_buf, st_send, st_recv, NY, ypos, at_y)

    for copy in copies[1:5]:
        copy.wait()

    angle = lax.rem(rot_ref[...] + inp_ref[...], NROT).astype(F32)
    rows_t = angle.shape[0]
    angle = jnp.concatenate([angle, jnp.zeros((LANES - rows_t, LANES), F32)], axis=0)
    angle_t[...] = angle.T.astype(BF16)

    def tilt_hot(b):
        tilt = jnp.concatenate(
            [tilt_ref[pl.ds(CUTS * b + h, 1), :] for h in range(CUTS)], axis=1
        )
        row = lax.broadcasted_iota(I32, (NTILT, CHUNK), 0)
        k_id = jnp.where(row < HALF, row, NTILT + HALF - 1 - row)
        return jnp.where(k_id == tilt, 1.0, 0.0).astype(BF16)

    row_pick = lax.broadcasted_iota(I32, (LANES, CHUNK), 0)
    lane_half = lax.div(lax.broadcasted_iota(I32, (LANES, CHUNK), 1), LANES)
    lane_turn = lax.rem(lax.broadcasted_iota(I32, (LANES, LANES), 1), NROT).astype(F32)

    def prepare_chunk(b, _):
        rows = chunk_rows(b)
        pick = jnp.where(row_pick == lane_half + CUTS * b, 1.0, 0.0).astype(BF16)
        spread = dot(angle_t[...], pick)
        hots = [
            jnp.where(spread[:, h * LANES : (h + 1) * LANES] == lane_turn, 1.0, 0.0).astype(BF16)
            for h in range(CUTS)
        ]
        ph_ref[rows, :] = dot(jnp.concatenate(hots, axis=0), phase_ref[...])
        e_high, e_low = split2(e_ref[rows, :])
        both = dot(tilt_hot(b), jnp.concatenate([e_high, e_low], axis=1))
        emass[b] = both[:, :LANES] + both[:, LANES:]
        return 0

    lax.fori_loop(0, chunks, prepare_chunk, 0)

    shared(st_buf, st_send, st_recv, NY, ypos, at_y)
    stats = [st_buf[p] for p in range(NY)]
    all_top = functools.reduce(jnp.maximum, [s[0:1] for s in stats])
    all_sum = functools.reduce(
        jnp.add, [s[1:2] * jnp.exp2(s[0:1] - all_top) for s in stats]
    )
    log_sum = jnp.log(all_sum)
    loglik_ref[...] = all_top * math.log(2.0) + log_sum
    scales = jnp.exp2((tops - all_top) - log_sum * LOG2E)
    cmax[pl.ds(0, chunks), :] = scales


    def weighted_stage(b):
        posterior = (e_ref[chunk_rows(b), :] * cmax[pl.ds(b, 1), :]).astype(BF16)
        raw_buf[...] = dot(jnp.concatenate([posterior, posterior], axis=1), shelled)

    def rotate_stage(b):
        rows = chunk_rows(b)
        real, imag = raw_buf[:, :LANES], raw_buf[:, LANES:]
        cosine, sine = ph_ref[rows, :LANES], ph_ref[rows, LANES:]
        for part, turned in enumerate((real * cosine + imag * sine, imag * cosine - real * sine)):
            high, low = split2(turned)
            high_buf[:, part * LANES : (part + 1) * LANES] = high
            low_buf[:, part * LANES : (part + 1) * LANES] = low

    def tilt_stage(b):
        hot = tilt_hot(b)
        return dot(hot, high_buf[...]) + dot(hot, low_buf[...])

    binned = jnp.zeros((NTILT, 2 * LANES), F32)
    for step in range(chunks + 2):
        if step >= 2:
            binned = binned + tilt_stage(step - 2)
        if 1 <= step <= chunks:
            rotate_stage(step - 1)
        if step < chunks:
            weighted_stage(step)
    bins_ref[0] = binned[:, :LANES]
    bins_ref[1] = binned[:, LANES:]

    copies[5].wait()

    sub8 = lax.broadcasted_iota(I32, (8, LANES), 0)
    lane8 = lax.broadcasted_iota(I32, (8, LANES), 1)
    even = lax.rem(sub8 + lane8, 2) == 0

    def project(k8, accs):
        accs = list(accs)
        for dk in range(8):
            k = k8 * 8 + dk
            for part in range(2):
                row = bins_ref[part, pl.ds(k, 1), :]
                mirror = bins_ref[part, pl.ds(HALF + k, 1), :]
                folded = jnp.where(even, row + mirror, row - mirror)
                for jb in range(LB):
                    accs[part * LB + jb] = (
                        accs[part * LB + jb] + lt[k, 8 * jb : 8 * jb + 8, :] * folded
                    )
        return tuple(accs)

    zero = jnp.zeros((8, LANES), F32)
    accs = lax.fori_loop(0, HALF // 8, project, (zero,) * (2 * LB))
    for q in range(2 * NYC):
        rhs_ref[q // 2, (q % 2) * 8 : (q % 2) * 8 + 8, :] = accs[q] if q < 2 * LB else zero

    r_yc[ycpos] = rhs_ref[ycpos]
    for d, p in enumerate(peers(NYC, ycpos)):
        remote(
            rhs_ref.at[p], r_yc.at[ycpos], ryc_send.at[d], ryc_recv.at[ycpos], at_yc(p)
        ).start()

    mass = jnp.zeros((NTILT, LANES), F32)
    for b in range(chunks):
        mass = mass + emass[b] * scales[b : b + 1]
    mass = jnp.broadcast_to(jnp.sum(mass, axis=1, keepdims=True), (NTILT, LANES))
    packed = jnp.zeros((8, LANES), F32)
    for q in range(4):
        for h in range(2):
            start = h * HALF + 8 * q
            packed = jnp.where(lax.div(lane, 16) == 2 * q + h, mass[start : start + 8], packed)
    m_zc[zcpos] = packed
    share(m_zc, mzc_send, mzc_recv, NZC, zcpos, at_zc)

    copies[6].wait()
    for jb in range(LB):
        for ib in range(LB):
            if jb <= ib:
                for r in range(8 if ib < LB - 1 else 1):
                    w_ref[ib * 8 + r, 8 * jb : 8 * jb + 8, :] = (
                        jnp.where(sub8 == r, 1.0, 0.0) if ib == jb else zero
                    )

    shared(r_yc, ryc_send, ryc_recv, NYC, ycpos, at_yc)
    r_x[xpos] = functools.reduce(jnp.add, [r_yc[p] for p in range(NYC)])
    share(r_x, rx_send, rx_recv, NX, xpos, at_x)

    shared(m_zc, mzc_send, mzc_recv, NZC, zcpos, at_zc)
    m_xy[xypos] = functools.reduce(jnp.add, [m_zc[p] for p in range(NZC)])
    share(m_xy, mxy_send, mxy_recv, NXY, xypos, at_xy)

    shared(r_x, rx_send, rx_recv, NX, xpos, at_x)
    r_z[zpos] = functools.reduce(jnp.add, [r_x[p] for p in range(NX)])
    share(r_z, rz_send, rz_recv, NZ, zpos, at_z)

    shared(m_xy, mxy_send, mxy_recv, NXY, xypos, at_xy)
    pm = functools.reduce(jnp.add, [m_xy[p] for p in range(NXY)])
    mean_mass = jnp.sum(jnp.sum(pm, axis=0, keepdims=True), axis=1, keepdims=True) / (
        16.0 * NTILT
    )
    first_half = lax.rem(lane, 32) < 16
    near = jnp.where(first_half, pm, pltpu.roll(pm, 16, 1))
    far = jnp.where(first_half, pltpu.roll(pm, LANES - 16, 1), pm)
    both_mass, diff_mass = near + far, near - far
    shell_lane = lax.div(lane, ORDERS)
    count = jnp.zeros((1, LANES), F32)
    for p in range(RADII):
        count = count + jnp.where(shell_lane == radius_ref[:, p : p + 1], 1.0, 0.0)
    ridge = (RIDGE * mean_mass) * (count + 1.0)
    sub_even = lax.rem(sub8, 2) == 0
    for k in range(8):
        plus, minus = both_mass[k : k + 1], diff_mass[k : k + 1]
        for parity in range(2):
            signed = jnp.where(sub_even, minus, plus) if parity else jnp.where(sub_even, plus, minus)
            for jb in range(LB):
                mlq[parity * 8 + k, 8 * jb : 8 * jb + 8, :] = (
                    lq[k, 8 * jb : 8 * jb + 8, :] * signed
                )
    for ib in range(LB):

        def gram_rows(h, _, ib=ib):
            group = 4 if ib < LB - 1 else 1
            first = ib * 8 + h * 4
            acc = [[zero] * LB for _ in range(group)]
            for k in range(8):
                rows = [lq[k, pl.ds(first + r, 1), :] for r in range(group)]
                for jb in range(ib, LB):
                    for parity in range(min(group, 2)):
                        term = mlq[parity * 8 + k, 8 * jb : 8 * jb + 8, :]
                        for r in range(parity, group, 2):
                            acc[r][jb] = acc[r][jb] + term * rows[r]
            for jb in range(ib, LB):
                for r in range(group):
                    v = acc[r][jb]
                    v = v + pltpu.roll(v, 32, 1)
                    v = v + pltpu.roll(v, 64, 1)
                    v = v * count
                    if jb == ib:
                        v = v + jnp.where(sub8 == h * 4 + r, ridge, 0.0)
                    a_ref[first + r, 8 * jb : 8 * jb + 8, :] = v
            return 0

        lax.fori_loop(0, 2 if ib < LB - 1 else 1, gram_rows, 0)

    shared(r_z, rz_send, rz_recv, NZ, zpos, at_z)
    r_ag[ycpos] = functools.reduce(jnp.add, [r_z[p] for p in range(NZ)])
    share(r_ag, rag_send, rag_recv, NYC, ycpos, at_yc)

    def blk(jb):
        return slice(8 * jb, 8 * jb + 8)

    for kb in range(LB):
        rows_here = 8 if kb < LB - 1 else 1
        for kk in range(rows_here):
            k = kb * 8 + kk
            rinv = 1.0 / a_ref[k, k : k + 1, :]
            dinv[k : k + 1, :] = rinv
            if k == LDEG:
                break
            upper = {jb: a_ref[k, blk(jb), :] for jb in range(kb, LB)}
            lower = {jb: w_ref[k, blk(jb), :] for jb in range(kb + 1)}
            factor = {jb: upper[jb] * rinv for jb in range(kb, LB)}
            for jb in range(kb, LB):
                pf_ref[kk, blk(jb), :] = factor[jb]
            for ii in range(kk + 1, rows_here):
                f = factor[kb][ii : ii + 1]
                for jb in range(kb, LB):
                    a_ref[kb * 8 + ii, blk(jb), :] -= f * upper[jb]
                for jb in range(kb + 1):
                    w_ref[kb * 8 + ii, blk(jb), :] -= f * lower[jb]
        for ib in range(kb + 1, LB):

            def trail(h, _, ib=ib, kb=kb):
                group = 4 if ib < LB - 1 else 1
                first = ib * 8 + h * 4
                f = [
                    [pf_ref[kk, pl.ds(first + r, 1), :] for r in range(group)] for kk in range(8)
                ]
                for ref, blocks in ((a_ref, range(ib, LB)), (w_ref, range(kb + 1))):
                    for jb in blocks:
                        v = [ref[first + r, blk(jb), :] for r in range(group)]
                        for kk in range(8):
                            u = ref[kb * 8 + kk, blk(jb), :]
                            v = [v[r] - f[kk][r] * u for r in range(group)]
                        for r in range(group):
                            ref[first + r, blk(jb), :] = v[r]
                return 0

            lax.fori_loop(0, 2 if ib < LB - 1 else 1, trail, 0)

    sent(st_buf, st_send, st_recv, NY, ypos, at_y)
    sent(m_zc, mzc_send, mzc_recv, NZC, zcpos, at_zc)
    sent(m_xy, mxy_send, mxy_recv, NXY, xypos, at_xy)
    for d, p in enumerate(peers(NYC, ycpos)):
        remote(
            rhs_ref.at[p], r_yc.at[ycpos], ryc_send.at[d], ryc_recv.at[ycpos], at_yc(p)
        ).wait_send()
    sent(r_x, rx_send, rx_recv, NX, xpos, at_x)
    sent(r_z, rz_send, rz_recv, NZ, zpos, at_z)
    shared(r_ag, rag_send, rag_recv, NYC, ycpos, at_yc)

    rhs = [r_ag[q // 2, (q % 2) * 8 : (q % 2) * 8 + 8, :] for q in range(2 * LB)]
    xs = [zero] * (2 * LB)
    for i in range(LROWS):
        ib = i // 8
        rows = [w_ref[i, blk(jb), :] for jb in range(ib + 1)]
        for part in range(2):
            t = rows[0] * rhs[part * LB]
            for jb in range(1, ib + 1):
                t = t + rows[jb] * rhs[part * LB + jb]
            s = jnp.sum(t, axis=0, keepdims=True) * dinv[i : i + 1, :]
            for jb in range(ib + 1):
                xs[part * LB + jb] = xs[part * LB + jb] + rows[jb] * s

    scale = math.sqrt(TEMPLATES)
    for q in range(2 * LB):
        out_ref[q // LB, blk(q % LB), :] = xs[q] * scale

    sent(r_ag, rag_send, rag_recv, NYC, ycpos, at_yc)


def arrange(x_ref, row_ref, out_ref, loglik_ref):
    loglik_ref[...] = row_ref[...]
    pad = jnp.zeros((LANES - LPAD, LANES), F32)
    for part in range(2):
        full = jnp.concatenate([x_ref[part], pad], axis=0).T
        for s in range(SHELLS):
            out_ref[:, s, part, :] = full[s * ORDERS : (s + 1) * ORDERS, :LROWS]


def body(images, templates, rotation, tilt, inplane, group, precision, radius_bin):
    t_count = templates.shape[0]
    rows = t_count // LANES
    chunks = t_count // CHUNK
    spread, packed, phases = constant_tables()
    vmem = pl.BlockSpec(memory_space=pltpu.VMEM)
    hbm = pl.BlockSpec(memory_space=pl.ANY)
    dma = pltpu.SemaphoreType.DMA
    solved, row = pl.pallas_call(
        kernel,
        out_shape=(
            pltpu.VMEM((2, LPAD, LANES), F32),
            pltpu.VMEM((1, LANES), F32),
        ),
        in_specs=[hbm, hbm, hbm, hbm, hbm, hbm, hbm, hbm, hbm, hbm, hbm],
        out_specs=(vmem, vmem),
        scratch_shapes=[
            pltpu.VMEM((rows, LANES), I32),
            pltpu.VMEM((rows, LANES), I32),
            pltpu.VMEM((rows, LANES), I32),
            pltpu.VMEM((1, LANES), I32),
            pltpu.VMEM((1, NGROUP), F32),
            pltpu.VMEM((1, RADII), I32),
            pltpu.VMEM(phases.shape, BF16),
            pltpu.VMEM(images.shape, BF16),
            pltpu.VMEM((CHUNK, 2 * LANES), F32),
            pltpu.VMEM((CHUNK, LANES), F32),
            pltpu.VMEM((CHUNK, 2 * LANES), BF16),
            pltpu.VMEM((CHUNK, 2 * LANES), BF16),
            pltpu.VMEM((t_count, COEFS), BF16),
            pltpu.VMEM((HALF, LPAD, LANES), F32),
            pltpu.VMEM((8, LPAD, LANES), F32),
            pltpu.VMEM((16, LPAD, LANES), F32),
            pltpu.VMEM((t_count, LANES), F32),
            pltpu.VMEM((t_count, 2 * LANES), F32),
            pltpu.VMEM((chunks, NTILT, LANES), F32),
            pltpu.VMEM((LANES, LANES), BF16),
            pltpu.VMEM((2 * chunks, LANES), F32),
            pltpu.VMEM((LPAD, LPAD, LANES), F32),
            pltpu.VMEM((LPAD, LPAD, LANES), F32),
            pltpu.VMEM((8, LPAD, LANES), F32),
            pltpu.VMEM((LPAD, LANES), F32),
            pltpu.VMEM((2, NTILT, LANES), F32),
            pltpu.VMEM((NYC, 16, LANES), F32),
            pltpu.VMEM((NY, 8, LANES), F32),
            pltpu.VMEM((NZC, 8, LANES), F32),
            pltpu.VMEM((NXY, 8, LANES), F32),
            pltpu.VMEM((NYC, 16, LANES), F32),
            pltpu.VMEM((NX, 16, LANES), F32),
            pltpu.VMEM((NZ, 16, LANES), F32),
            pltpu.VMEM((NYC, 16, LANES), F32),
            dma((chunks,)),
            dma((10,)),
            dma((NY - 1,)),
            dma((NY,)),
            dma((NZC - 1,)),
            dma((NZC,)),
            dma((NXY - 1,)),
            dma((NXY,)),
            dma((NYC - 1,)),
            dma((NYC,)),
            dma((NX - 1,)),
            dma((NX,)),
            dma((NZ - 1,)),
            dma((NZ,)),
            dma((NYC - 1,)),
            dma((NYC,)),
        ],
        compiler_params=pltpu.CompilerParams(collective_id=0, has_side_effects=True),
        name="estep",
    )(
        tilt.reshape(rows, LANES),
        rotation.reshape(rows, LANES),
        inplane.reshape(rows, LANES),
        group.reshape(1, LANES),
        precision.reshape(1, NGROUP),
        radius_bin.reshape(1, RADII),
        jnp.asarray(phases),
        images,
        jnp.asarray(spread),
        jnp.asarray(packed),
        templates,
    )
    coeffs, loglik = pl.pallas_call(
        arrange,
        out_shape=(
            jax.ShapeDtypeStruct((ORDERS, SHELLS, 2, LROWS), F32),
            jax.ShapeDtypeStruct((1, LANES), F32),
        ),
        in_specs=[vmem, vmem],
        out_specs=(vmem, vmem),
        name="arrange",
    )(
        pltpu.with_memory_space_constraint(solved, pltpu.VMEM),
        pltpu.with_memory_space_constraint(row, pltpu.VMEM),
    )
    return coeffs, loglik.reshape(LANES)


def solution(mesh):
    in_specs = (
        P("img", None),
        P(("tpa", "tpb"), None),
        P(("tpa", "tpb")),
        P(("tpa", "tpb")),
        P(("tpa", "tpb")),
        P("img"),
        P(),
        P(),
    )
    out_specs = (P(), P("img"))
    return jax.shard_map(body, mesh=mesh, in_specs=in_specs, out_specs=out_specs, check_vma=False)
```

```python
import functools
import math

import jax
import jax.numpy as jnp
import numpy as np
from jax import lax
from jax.experimental import pallas as pl
from jax.experimental.pallas import tpu as pltpu
from jax.sharding import PartitionSpec as P

TEMPLATES = 16384
ORDERS = 32
RADII = 8
COEFS = 512
LDEG = 48
SHELLS = 4
NTILT = 64
NROT = 32
NGROUP = 16
RIDGE = 0.05
LOG2E = math.log2(math.e)

NX, NZ, NCORE, NY = 4, 8, 2, 4
NYC = NY * NCORE
NZC = NZ * NCORE
NXY = NX * NY
HALF = NTILT // 2
LANES = 128
LB = 7
LPAD = 8 * LB
LROWS = LDEG + 1
CHUNK = 512
CUTS = CHUNK // LANES
F32, BF16, I32 = jnp.float32, jnp.bfloat16, jnp.int32
MESH = pl.DeviceIdType.MESH


def legendre_table():
    theta = np.pi * (np.arange(NTILT) + 0.5) / NTILT
    cosine, sine = np.cos(theta)[:, None], np.sin(theta)
    orders = np.arange(ORDERS, dtype=np.float64)[None, :]
    diagonal = [np.full((NTILT,), (4.0 * np.pi) ** -0.5)]
    for m in range(1, ORDERS):
        diagonal.append(-np.sqrt((2 * m + 1) / (2.0 * m)) * sine * diagonal[-1])
    corner = np.stack(diagonal, axis=1)
    before = np.zeros((NTILT, ORDERS))
    latest = np.zeros((NTILT, ORDERS))
    columns = []
    for degree in range(LDEG + 1):
        low = float(degree - 1)
        factor = np.sqrt(
            max(4.0 * degree * degree - 1.0, 1.0)
            / np.maximum(degree * degree - orders * orders, 1.0)
        )
        factor_prev = np.sqrt(
            max(4.0 * low * low - 1.0, 1.0) / np.maximum(low * low - orders * orders, 1.0)
        )
        recurred = factor * (cosine * latest - before / factor_prev)
        current = np.where(orders == degree, corner, np.where(orders < degree, recurred, 0.0))
        columns.append(current)
        before, latest = latest, current
    return np.stack(columns, axis=2)


def constant_tables():
    legendre = legendre_table().transpose(0, 2, 1)
    padded = np.zeros((HALF, LPAD, ORDERS))
    padded[:, :LROWS] = legendre[:HALF]
    spread = np.tile(padded, (1, 1, SHELLS)).astype(np.float32)
    packed = np.concatenate([padded[q * 8 : q * 8 + 8] for q in range(4)], axis=2)
    packed = packed.astype(np.float32)
    step = np.arange(NROT)[:, None] * np.arange(ORDERS)[None, :] % NROT
    turn = 2.0 * np.pi * step / NROT
    both = np.concatenate([np.tile(np.cos(turn), (1, 4)), np.tile(np.sin(turn), (1, 4))], axis=1)
    rest, terms = both, []
    for _ in range(3):
        term = rest.astype(np.float32).astype(jnp.bfloat16)
        terms.append(term)
        rest = rest - term.astype(np.float64)
    terms.append(np.zeros_like(terms[0]))
    phases = np.concatenate(terms, axis=0)
    return spread, packed, phases


def split2(value):
    high = value.astype(BF16)
    return high, (value - high.astype(F32)).astype(BF16)


def dot(a, b):
    return lax.dot_general(a, b, (((1,), (0,)), ((), ())), preferred_element_type=F32)


def dot_t(a, b):
    return lax.dot_general(a, b, (((1,), (1,)), ((), ())), preferred_element_type=F32)


def kernel(
    tilt_hbm,
    rot_hbm,
    inp_hbm,
    group_hbm,
    prec_hbm,
    radius_hbm,
    phase_hbm,
    images_hbm,
    lt_hbm,
    lq_hbm,
    templates_hbm,
    out_ref,
    loglik_ref,
    tilt_ref,
    rot_ref,
    inp_ref,
    group_ref,
    prec_ref,
    radius_ref,
    phase_ref,
    images_ref,
    raw_buf,
    score_buf,
    high_buf,
    low_buf,
    tpl,
    lt,
    lq,
    mlq,
    e_ref,
    ph_ref,
    emass,
    angle_t,
    cmax,
    a_ref,
    w_ref,
    pf_ref,
    dinv,
    bins_ref,
    rhs_ref,
    st_buf,
    m_zc,
    m_xy,
    r_yc,
    r_x,
    r_z,
    r_ag,
    tpl_sem,
    tab_sem,
    st_send,
    st_recv,
    mzc_send,
    mzc_recv,
    mxy_send,
    mxy_recv,
    ryc_send,
    ryc_recv,
    rx_send,
    rx_recv,
    rz_send,
    rz_recv,
    rag_send,
    rag_recv,
):
    t_count = templates_hbm.shape[0]
    chunks = t_count // CHUNK
    img = lax.axis_index("img")
    tpa = lax.axis_index("tpa")
    tpb = lax.axis_index("tpb")
    core = lax.rem(img, NCORE)
    zpos = lax.rem(lax.div(img, NCORE), NZ)
    xpos = lax.div(img, NCORE * NZ)
    ypos = tpb * 2 + tpa
    ycpos = core * NY + ypos

    zcpos = zpos * NCORE + core
    xypos = xpos * NY + ypos
    chip = img - core
    column = img - zcpos

    def device(at_img, y):
        return {"img": at_img, "tpa": lax.rem(y, 2), "tpb": lax.div(y, 2)}

    def at_y(p):
        return device(img, p)

    def at_yc(p):
        return device(chip + lax.div(p, NY), lax.rem(p, NY))

    def at_x(p):
        return {"img": p * NZC + zcpos, "tpa": tpa, "tpb": tpb}

    def at_z(p):
        return {"img": column + p * NCORE + core, "tpa": tpa, "tpb": tpb}

    def at_zc(p):
        return {"img": column + p, "tpa": tpa, "tpb": tpb}

    def at_xy(p):
        return device(lax.div(p, NY) * NZC + zcpos, lax.rem(p, NY))

    def peers(n, me):
        if n == NYC and me is ycpos:
            steps = (2, 6, 1, 3, 5, 7, 4)
        else:
            steps = sorted(range(1, n), key=lambda d: -min(d, n - d))
        return [lax.rem(me + d, n) for d in steps]

    def remote(src, dst, send, recv, device):
        return pltpu.make_async_remote_copy(
            src_ref=src,
            dst_ref=dst,
            send_sem=send,
            recv_sem=recv,
            device_id=device,
            device_id_type=MESH,
        )

    def share(buf, send, recv, n, me, at):
        for d, p in enumerate(peers(n, me)):
            remote(buf.at[me], buf.at[me], send.at[d], recv.at[me], at(p)).start()

    def shared(buf, send, recv, n, me, at):
        for d, p in enumerate(peers(n, me)):
            remote(buf.at[p], buf.at[p], send.at[d], recv.at[p], at(p)).wait_recv()

    def sent(buf, send, recv, n, me, at):
        for d, p in enumerate(peers(n, me)):
            remote(buf.at[me], buf.at[me], send.at[d], recv.at[me], at(p)).wait_send()

    def tpl_copy(b):
        rows = pl.ds(b * CHUNK, CHUNK)
        return pltpu.make_async_copy(templates_hbm.at[rows], tpl.at[rows], tpl_sem.at[b])

    operands = (
        (images_hbm, images_ref),
        (tilt_hbm, tilt_ref),
        (rot_hbm, rot_ref),
        (inp_hbm, inp_ref),
        (phase_hbm, phase_ref),
        (lt_hbm, lt),
        (lq_hbm, lq),
        (group_hbm, group_ref),
        (prec_hbm, prec_ref),
        (radius_hbm, radius_ref),
    )
    copies = [
        pltpu.make_async_copy(src, dst, tab_sem.at[i]) for i, (src, dst) in enumerate(operands)
    ]
    for i in (7, 8, 9, 0):
        copies[i].start()
    for b in range(chunks):
        tpl_copy(b).start()
    for copy in copies[1:7]:
        copy.start()

    barrier = pltpu.get_barrier_semaphore()
    greeted = [at_zc(p) for p in peers(NZC, zcpos)] + [at_xy(p) for p in peers(NXY, xypos)]
    greeted += [device(chip + 1 - core, p) for p in peers(NY, ypos)]
    for target in greeted:
        pl.semaphore_signal(barrier, inc=1, device_id=target, device_id_type=MESH)

    lane = lax.broadcasted_iota(I32, (1, LANES), 1)

    for i in (7, 8, 9, 0):
        copies[i].wait()
    group = group_ref[...]
    weight = jnp.zeros((1, LANES), F32)
    for g in range(NGROUP):
        weight = jnp.where(group == g, prec_ref[:, g : g + 1], weight)
    weight = weight * (COEFS ** -0.5 * LOG2E)

    r_id = lax.broadcasted_iota(I32, (16, LANES), 0)
    l_id = lax.broadcasted_iota(I32, (16, LANES), 1)
    order_at = l_id
    for p in range(RADII):
        order_at = jnp.where(lax.div(r_id, 2) == p, l_id - ORDERS * radius_ref[:, p : p + 1], order_at)
    order_of = [jnp.where(lax.rem(r_id, 2) == part, order_at, -1) for part in range(2)]
    select = jnp.concatenate(
        [
            jnp.concatenate([jnp.where(o == m, 1.0, 0.0).astype(BF16) for o in order_of], axis=1)
            for m in range(ORDERS)
        ],
        axis=0,
    )
    images = images_ref[...]
    img_high, img_low = split2(dot(images, select))
    shelled = jnp.concatenate([img_high, img_low], axis=0)

    def chunk_rows(b):
        return pl.ds(b * CHUNK if isinstance(b, int) else pl.multiple_of(b * CHUNK, CHUNK), CHUNK)

    def raw_stage(b):
        raw_buf[:, :LANES] = dot_t(tpl[chunk_rows(b), :], images)

    def score_stage(b):
        wide = tpl[chunk_rows(b), :].astype(F32)
        half = 0.5 * jnp.sum(wide * wide, axis=1, keepdims=True)
        score = (raw_buf[:, :LANES] - half) * weight
        score_buf[...] = score
        cmax[pl.ds(b, 1), :] = jnp.max(score, axis=0, keepdims=True)

    def exp_stage(b):
        e = jnp.exp2(score_buf[...] - cmax[pl.ds(b, 1), :])
        e_ref[chunk_rows(b), :] = e
        cmax[pl.ds(chunks + b, 1), :] = jnp.sum(e, axis=0, keepdims=True)

    waits = {0: (0,), 1: (1,), 2: (2, 3), 4: tuple(range(4, chunks))}
    for step in range(chunks + 2):
        for b in waits.get(step, ()):
            tpl_copy(b).wait()
        if step >= 2:
            exp_stage(step - 2)
        if 1 <= step <= chunks:
            score_stage(step - 1)
        if step < chunks:
            raw_stage(step)

    tops = cmax[pl.ds(0, chunks), :]
    sums = cmax[pl.ds(chunks, chunks), :]
    top = jnp.max(tops, axis=0, keepdims=True)
    total = jnp.sum(sums * jnp.exp2(tops - top), axis=0, keepdims=True)
    row8 = lax.broadcasted_iota(I32, (8, LANES), 0)
    st_buf[ypos] = jnp.where(row8 == 0, top, total)

    pl.semaphore_wait(barrier, (NZC - 1) + (NXY - 1) + (NY - 1))
    share(st_buf, st_send, st_recv, NY, ypos, at_y)

    for copy in copies[1:5]:
        copy.wait()

    angle = lax.rem(rot_ref[...] + inp_ref[...], NROT).astype(F32)
    rows_t = angle.shape[0]
    angle = jnp.concatenate([angle, jnp.zeros((LANES - rows_t, LANES), F32)], axis=0)
    angle_t[...] = angle.T.astype(BF16)

    def tilt_hot(b):
        tilt = jnp.concatenate(
            [tilt_ref[pl.ds(CUTS * b + h, 1), :] for h in range(CUTS)], axis=1
        )
        row = lax.broadcasted_iota(I32, (NTILT, CHUNK), 0)
        k_id = jnp.where(row < HALF, row, NTILT + HALF - 1 - row)
        return jnp.where(k_id == tilt, 1.0, 0.0).astype(BF16)

    row_pick = lax.broadcasted_iota(I32, (LANES, CHUNK), 0)
    lane_half = lax.div(lax.broadcasted_iota(I32, (LANES, CHUNK), 1), LANES)
    lane_turn = lax.rem(lax.broadcasted_iota(I32, (LANES, LANES), 1), NROT).astype(F32)

    def prepare_chunk(b, _):
        rows = chunk_rows(b)
        pick = jnp.where(row_pick == lane_half + CUTS * b, 1.0, 0.0).astype(BF16)
        spread = dot(angle_t[...], pick)
        hots = [
            jnp.where(spread[:, h * LANES : (h + 1) * LANES] == lane_turn, 1.0, 0.0).astype(BF16)
            for h in range(CUTS)
        ]
        ph_ref[rows, :] = dot(jnp.concatenate(hots, axis=0), phase_ref[...])
        e_high, e_low = split2(e_ref[rows, :])
        both = dot(tilt_hot(b), jnp.concatenate([e_high, e_low], axis=1))
        emass[b] = both[:, :LANES] + both[:, LANES:]
        return 0

    lax.fori_loop(0, chunks, prepare_chunk, 0)

    shared(st_buf, st_send, st_recv, NY, ypos, at_y)
    stats = [st_buf[p] for p in range(NY)]
    all_top = functools.reduce(jnp.maximum, [s[0:1] for s in stats])
    all_sum = functools.reduce(
        jnp.add, [s[1:2] * jnp.exp2(s[0:1] - all_top) for s in stats]
    )
    log_sum = jnp.log(all_sum)
    loglik_ref[...] = all_top * math.log(2.0) + log_sum
    scales = jnp.exp2((tops - all_top) - log_sum * LOG2E)
    cmax[pl.ds(0, chunks), :] = scales


    def weighted_stage(b):
        posterior = (e_ref[chunk_rows(b), :] * cmax[pl.ds(b, 1), :]).astype(BF16)
        raw_buf[...] = dot(jnp.concatenate([posterior, posterior], axis=1), shelled)

    def rotate_stage(b):
        rows = chunk_rows(b)
        real, imag = raw_buf[:, :LANES], raw_buf[:, LANES:]
        cosine, sine = ph_ref[rows, :LANES], ph_ref[rows, LANES:]
        for part, turned in enumerate((real * cosine + imag * sine, imag * cosine - real * sine)):
            high, low = split2(turned)
            high_buf[:, part * LANES : (part + 1) * LANES] = high
            low_buf[:, part * LANES : (part + 1) * LANES] = low

    def tilt_stage(b):
        hot = tilt_hot(b)
        return dot(hot, high_buf[...]) + dot(hot, low_buf[...])

    binned = jnp.zeros((NTILT, 2 * LANES), F32)
    for step in range(chunks + 2):
        if step >= 2:
            binned = binned + tilt_stage(step - 2)
        if 1 <= step <= chunks:
            rotate_stage(step - 1)
        if step < chunks:
            weighted_stage(step)
    bins_ref[0] = binned[:, :LANES]
    bins_ref[1] = binned[:, LANES:]

    copies[5].wait()

    sub8 = lax.broadcasted_iota(I32, (8, LANES), 0)
    lane8 = lax.broadcasted_iota(I32, (8, LANES), 1)
    even = lax.rem(sub8 + lane8, 2) == 0

    def project(k8, accs):
        accs = list(accs)
        for dk in range(8):
            k = k8 * 8 + dk
            for part in range(2):
                row = bins_ref[part, pl.ds(k, 1), :]
                mirror = bins_ref[part, pl.ds(HALF + k, 1), :]
                folded = jnp.where(even, row + mirror, row - mirror)
                for jb in range(LB):
                    accs[part * LB + jb] = (
                        accs[part * LB + jb] + lt[k, 8 * jb : 8 * jb + 8, :] * folded
                    )
        return tuple(accs)

    zero = jnp.zeros((8, LANES), F32)
    accs = lax.fori_loop(0, HALF // 8, project, (zero,) * (2 * LB))
    for q in range(2 * NYC):
        rhs_ref[q // 2, (q % 2) * 8 : (q % 2) * 8 + 8, :] = accs[q] if q < 2 * LB else zero

    r_yc[ycpos] = rhs_ref[ycpos]
    for d, p in enumerate(peers(NYC, ycpos)):
        remote(
            rhs_ref.at[p], r_yc.at[ycpos], ryc_send.at[d], ryc_recv.at[ycpos], at_yc(p)
        ).start()

    mass = jnp.zeros((NTILT, LANES), F32)
    for b in range(chunks):
        mass = mass + emass[b] * scales[b : b + 1]
    mass = jnp.broadcast_to(jnp.sum(mass, axis=1, keepdims=True), (NTILT, LANES))
    packed = jnp.zeros((8, LANES), F32)
    for q in range(4):
        for h in range(2):
            start = h * HALF + 8 * q
            packed = jnp.where(lax.div(lane, 16) == 2 * q + h, mass[start : start + 8], packed)
    m_zc[zcpos] = packed
    share(m_zc, mzc_send, mzc_recv, NZC, zcpos, at_zc)

    copies[6].wait()
    for jb in range(LB):
        for ib in range(LB):
            if jb <= ib:
                for r in range(8 if ib < LB - 1 else 1):
                    w_ref[ib * 8 + r, 8 * jb : 8 * jb + 8, :] = (
                        jnp.where(sub8 == r, 1.0, 0.0) if ib == jb else zero
                    )

    shared(r_yc, ryc_send, ryc_recv, NYC, ycpos, at_yc)
    r_x[xpos] = functools.reduce(jnp.add, [r_yc[p] for p in range(NYC)])
    share(r_x, rx_send, rx_recv, NX, xpos, at_x)

    shared(m_zc, mzc_send, mzc_recv, NZC, zcpos, at_zc)
    m_xy[xypos] = functools.reduce(jnp.add, [m_zc[p] for p in range(NZC)])
    share(m_xy, mxy_send, mxy_recv, NXY, xypos, at_xy)

    shared(r_x, rx_send, rx_recv, NX, xpos, at_x)
    r_z[zpos] = functools.reduce(jnp.add, [r_x[p] for p in range(NX)])
    share(r_z, rz_send, rz_recv, NZ, zpos, at_z)

    shared(m_xy, mxy_send, mxy_recv, NXY, xypos, at_xy)
    pm = functools.reduce(jnp.add, [m_xy[p] for p in range(NXY)])
    mean_mass = jnp.sum(jnp.sum(pm, axis=0, keepdims=True), axis=1, keepdims=True) / (
        16.0 * NTILT
    )
    first_half = lax.rem(lane, 32) < 16
    near = jnp.where(first_half, pm, pltpu.roll(pm, 16, 1))
    far = jnp.where(first_half, pltpu.roll(pm, LANES - 16, 1), pm)
    both_mass, diff_mass = near + far, near - far
    shell_lane = lax.div(lane, ORDERS)
    count = jnp.zeros((1, LANES), F32)
    for p in range(RADII):
        count = count + jnp.where(shell_lane == radius_ref[:, p : p + 1], 1.0, 0.0)
    ridge = (RIDGE * mean_mass) * (count + 1.0)
    sub_even = lax.rem(sub8, 2) == 0
    for k in range(8):
        plus, minus = both_mass[k : k + 1], diff_mass[k : k + 1]
        for parity in range(2):
            signed = jnp.where(sub_even, minus, plus) if parity else jnp.where(sub_even, plus, minus)
            for jb in range(LB):
                mlq[parity * 8 + k, 8 * jb : 8 * jb + 8, :] = (
                    lq[k, 8 * jb : 8 * jb + 8, :] * signed
                )
    for ib in range(LB):

        def gram_rows(h, _, ib=ib):
            group = 4 if ib < LB - 1 else 1
            first = ib * 8 + h * 4
            acc = [[zero] * LB for _ in range(group)]
            for k in range(8):
                rows = [lq[k, pl.ds(first + r, 1), :] for r in range(group)]
                for jb in range(ib, LB):
                    for parity in range(min(group, 2)):
                        term = mlq[parity * 8 + k, 8 * jb : 8 * jb + 8, :]
                        for r in range(parity, group, 2):
                            acc[r][jb] = acc[r][jb] + term * rows[r]
            for jb in range(ib, LB):
                for r in range(group):
                    v = acc[r][jb]
                    v = v + pltpu.roll(v, 32, 1)
                    v = v + pltpu.roll(v, 64, 1)
                    v = v * count
                    if jb == ib:
                        v = v + jnp.where(sub8 == h * 4 + r, ridge, 0.0)
                    a_ref[first + r, 8 * jb : 8 * jb + 8, :] = v
            return 0

        lax.fori_loop(0, 2 if ib < LB - 1 else 1, gram_rows, 0)
        if ib == 2:
            shared(r_z, rz_send, rz_recv, NZ, zpos, at_z)
            r_ag[ycpos] = functools.reduce(jnp.add, [r_z[p] for p in range(NZ)])
            share(r_ag, rag_send, rag_recv, NYC, ycpos, at_yc)

    def blk(jb):
        return slice(8 * jb, 8 * jb + 8)

    for kb in range(LB):
        rows_here = 8 if kb < LB - 1 else 1
        for kk in range(rows_here):
            k = kb * 8 + kk
            rinv = 1.0 / a_ref[k, k : k + 1, :]
            dinv[k : k + 1, :] = rinv
            if k == LDEG:
                break
            upper = {jb: a_ref[k, blk(jb), :] for jb in range(kb, LB)}
            lower = {jb: w_ref[k, blk(jb), :] for jb in range(kb + 1)}
            factor = {jb: upper[jb] * rinv for jb in range(kb, LB)}
            for jb in range(kb, LB):
                pf_ref[kk, blk(jb), :] = factor[jb]
            for ii in range(kk + 1, rows_here):
                f = factor[kb][ii : ii + 1]
                for jb in range(kb, LB):
                    a_ref[kb * 8 + ii, blk(jb), :] -= f * upper[jb]
                for jb in range(kb + 1):
                    w_ref[kb * 8 + ii, blk(jb), :] -= f * lower[jb]
        for ib in range(kb + 1, LB):

            def trail(h, _, ib=ib, kb=kb):
                group = 4 if ib < LB - 1 else 1
                first = ib * 8 + h * 4
                f = [
                    [pf_ref[kk, pl.ds(first + r, 1), :] for r in range(group)] for kk in range(8)
                ]
                for ref, blocks in ((a_ref, range(ib, LB)), (w_ref, range(kb + 1))):
                    for jb in blocks:
                        v = [ref[first + r, blk(jb), :] for r in range(group)]
                        for kk in range(8):
                            u = ref[kb * 8 + kk, blk(jb), :]
                            v = [v[r] - f[kk][r] * u for r in range(group)]
                        for r in range(group):
                            ref[first + r, blk(jb), :] = v[r]
                return 0

            lax.fori_loop(0, 2 if ib < LB - 1 else 1, trail, 0)

    sent(st_buf, st_send, st_recv, NY, ypos, at_y)
    sent(m_zc, mzc_send, mzc_recv, NZC, zcpos, at_zc)
    sent(m_xy, mxy_send, mxy_recv, NXY, xypos, at_xy)
    for d, p in enumerate(peers(NYC, ycpos)):
        remote(
            rhs_ref.at[p], r_yc.at[ycpos], ryc_send.at[d], ryc_recv.at[ycpos], at_yc(p)
        ).wait_send()
    sent(r_x, rx_send, rx_recv, NX, xpos, at_x)
    sent(r_z, rz_send, rz_recv, NZ, zpos, at_z)
    shared(r_ag, rag_send, rag_recv, NYC, ycpos, at_yc)

    rhs = [r_ag[q // 2, (q % 2) * 8 : (q % 2) * 8 + 8, :] for q in range(2 * LB)]
    xs = [zero] * (2 * LB)
    for i in range(LROWS):
        ib = i // 8
        rows = [w_ref[i, blk(jb), :] for jb in range(ib + 1)]
        for part in range(2):
            t = rows[0] * rhs[part * LB]
            for jb in range(1, ib + 1):
                t = t + rows[jb] * rhs[part * LB + jb]
            s = jnp.sum(t, axis=0, keepdims=True) * dinv[i : i + 1, :]
            for jb in range(ib + 1):
                xs[part * LB + jb] = xs[part * LB + jb] + rows[jb] * s

    scale = math.sqrt(TEMPLATES)
    for q in range(2 * LB):
        out_ref[q // LB, blk(q % LB), :] = xs[q] * scale

    sent(r_ag, rag_send, rag_recv, NYC, ycpos, at_yc)


def arrange(x_ref, row_ref, out_ref, loglik_ref):
    loglik_ref[...] = row_ref[...]
    pad = jnp.zeros((LANES - LPAD, LANES), F32)
    for part in range(2):
        full = jnp.concatenate([x_ref[part], pad], axis=0).T
        for s in range(SHELLS):
            out_ref[:, s, part, :] = full[s * ORDERS : (s + 1) * ORDERS, :LROWS]


def body(images, templates, rotation, tilt, inplane, group, precision, radius_bin):
    t_count = templates.shape[0]
    rows = t_count // LANES
    chunks = t_count // CHUNK
    spread, packed, phases = constant_tables()
    vmem = pl.BlockSpec(memory_space=pltpu.VMEM)
    hbm = pl.BlockSpec(memory_space=pl.ANY)
    dma = pltpu.SemaphoreType.DMA
    solved, row = pl.pallas_call(
        kernel,
        out_shape=(
            pltpu.VMEM((2, LPAD, LANES), F32),
            pltpu.VMEM((1, LANES), F32),
        ),
        in_specs=[hbm, hbm, hbm, hbm, hbm, hbm, hbm, hbm, hbm, hbm, hbm],
        out_specs=(vmem, vmem),
        scratch_shapes=[
            pltpu.VMEM((rows, LANES), I32),
            pltpu.VMEM((rows, LANES), I32),
            pltpu.VMEM((rows, LANES), I32),
            pltpu.VMEM((1, LANES), I32),
            pltpu.VMEM((1, NGROUP), F32),
            pltpu.VMEM((1, RADII), I32),
            pltpu.VMEM(phases.shape, BF16),
            pltpu.VMEM(images.shape, BF16),
            pltpu.VMEM((CHUNK, 2 * LANES), F32),
            pltpu.VMEM((CHUNK, LANES), F32),
            pltpu.VMEM((CHUNK, 2 * LANES), BF16),
            pltpu.VMEM((CHUNK, 2 * LANES), BF16),
            pltpu.VMEM((t_count, COEFS), BF16),
            pltpu.VMEM((HALF, LPAD, LANES), F32),
            pltpu.VMEM((8, LPAD, LANES), F32),
            pltpu.VMEM((16, LPAD, LANES), F32),
            pltpu.VMEM((t_count, LANES), F32),
            pltpu.VMEM((t_count, 2 * LANES), F32),
            pltpu.VMEM((chunks, NTILT, LANES), F32),
            pltpu.VMEM((LANES, LANES), BF16),
            pltpu.VMEM((2 * chunks, LANES), F32),
            pltpu.VMEM((LPAD, LPAD, LANES), F32),
            pltpu.VMEM((LPAD, LPAD, LANES), F32),
            pltpu.VMEM((8, LPAD, LANES), F32),
            pltpu.VMEM((LPAD, LANES), F32),
            pltpu.VMEM((2, NTILT, LANES), F32),
            pltpu.VMEM((NYC, 16, LANES), F32),
            pltpu.VMEM((NY, 8, LANES), F32),
            pltpu.VMEM((NZC, 8, LANES), F32),
            pltpu.VMEM((NXY, 8, LANES), F32),
            pltpu.VMEM((NYC, 16, LANES), F32),
            pltpu.VMEM((NX, 16, LANES), F32),
            pltpu.VMEM((NZ, 16, LANES), F32),
            pltpu.VMEM((NYC, 16, LANES), F32),
            dma((chunks,)),
            dma((10,)),
            dma((NY - 1,)),
            dma((NY,)),
            dma((NZC - 1,)),
            dma((NZC,)),
            dma((NXY - 1,)),
            dma((NXY,)),
            dma((NYC - 1,)),
            dma((NYC,)),
            dma((NX - 1,)),
            dma((NX,)),
            dma((NZ - 1,)),
            dma((NZ,)),
            dma((NYC - 1,)),
            dma((NYC,)),
        ],
        compiler_params=pltpu.CompilerParams(collective_id=0, has_side_effects=True),
        name="estep",
    )(
        tilt.reshape(rows, LANES),
        rotation.reshape(rows, LANES),
        inplane.reshape(rows, LANES),
        group.reshape(1, LANES),
        precision.reshape(1, NGROUP),
        radius_bin.reshape(1, RADII),
        jnp.asarray(phases),
        images,
        jnp.asarray(spread),
        jnp.asarray(packed),
        templates,
    )
    coeffs, loglik = pl.pallas_call(
        arrange,
        out_shape=(
            jax.ShapeDtypeStruct((ORDERS, SHELLS, 2, LROWS), F32),
            jax.ShapeDtypeStruct((1, LANES), F32),
        ),
        in_specs=[vmem, vmem],
        out_specs=(vmem, vmem),
        name="arrange",
    )(
        pltpu.with_memory_space_constraint(solved, pltpu.VMEM),
        pltpu.with_memory_space_constraint(row, pltpu.VMEM),
    )
    return coeffs, loglik.reshape(LANES)


def solution(mesh):
    in_specs = (
        P("img", None),
        P(("tpa", "tpb"), None),
        P(("tpa", "tpb")),
        P(("tpa", "tpb")),
        P(("tpa", "tpb")),
        P("img"),
        P(),
        P(),
    )
    out_specs = (P(), P("img"))
    return jax.shard_map(body, mesh=mesh, in_specs=in_specs, out_specs=out_specs, check_vma=False)
```
